32 devices in a mesh: rep: 2 (over y), step: 4 (over z), patch: 4 (over x, core).
Axes of the slice: x: 2, y: 2, z: 4, core: 2. Of those that a mesh axis runs over, the one named last changes fastest.
Arguments:
- latent_old: float32 [8, 1024, 64], P(('rep', 'step'), 'patch'), parts along dimension 0, may hold values from -6 to 6
- noise_start: float32 [2048, 64], P(('rep', 'patch')), parts along dimension 0, may hold values from -6 to 6
- step_index: int32 [8], P(('rep', 'step')), parts along dimension 0, may hold values from 0 to 998
- sigma_table: float32 [1000], replicated, may hold values from 0.02 to 1
- mod_weight: bfloat16 [256, 9216], replicated, may hold values from -0.375 to 0.375
- embed_weight: bfloat16 [64, 3072], replicated, may hold values from -0.75 to 0.75
- embed_bias: float32 [3072], replicated, may hold values from -3 to 3
- query_weight: bfloat16 [3072, 1536], P('step'), may hold values from -0.109375 to 0.109375
- query_gain: float32 [128], replicated, may hold values from 0.1 to 1.9
- stale_keys: bfloat16 [8, 1280, 1536], P(('rep', 'step'), 'patch'), parts along dimension 0, may hold values from -640 to 640
- stale_values: bfloat16 [8, 1280, 1536], P(('rep', 'step'), 'patch'), parts along dimension 0, may hold values from -6 to 6
- out_weight: bfloat16 [3072, 1536], P('step'), may hold values from -0.3125 to 0.3125
- final_weight: bfloat16 [3072, 64], replicated, may hold values from -0.109375 to 0.109375
Outputs:
- latent_new: float32 [8, 1024, 64], P(('rep', 'step'), 'patch'), parts along dimension 0
The draws below stay inside these ranges and needn't reach their ends.
There are 2 independent parts, one for each index of `rep`. The reference program is written for one: setup_inputs(seed, part) draws one part's arguments, and reference() takes and returns one part's arrays. A program takes and returns all parts, laid end to end along the dimension named above; an argument that names none is the same for every part. Nothing has to cross between parts.
All inputs are finite; a program needn't handle non-finite values.
Results may differ from the reference program's by a relative error of at most 0.012.
The reference program's roundings to bfloat16 on the way count: a program that leaves them out, or rounds other values in their place, can miss the bound.
Values may be sent and summed in bfloat16 or wider, within the bound.
A program may use at most 128 MiB of HBM per device.

```python
import math
import jax
import jax.numpy as jnp
from jax import lax

D = 3072
HEAD = 128
C = 64
FREQ = 256
HEADS = 12
TABLE = 1000
STEPS = 4
TOKENS = 1024
KEYS = 1280


def draw_stale_keys(key, part):
    key_base = jax.random.fold_in(jax.random.fold_in(key, 11), 0)
    width = HEADS * HEAD
    base = 2.5 * jnp.clip(jax.random.normal(key_base, (STEPS, KEYS, width), jnp.float32), -6.0, 6.0)
    return base.astype(jnp.bfloat16)


def with_ends(entries, key, smallest, largest):
    spot = [jax.random.randint(jax.random.fold_in(key, axis), (), 0, length) for axis, length in enumerate(entries.shape)]
    longest = entries.shape.index(max(entries.shape))
    beside = spot[:longest] + [(spot[longest] + 1) % entries.shape[longest]] + spot[longest + 1:]
    return entries.at[tuple(spot)].set(smallest).at[tuple(beside)].set(largest)


def block_scale(rng, dims, cuts, least, largest):
    level = 1.0
    for axis_at, blocks in cuts:
        heights = jax.random.uniform(jax.random.fold_in(jax.random.fold_in(rng, 6), axis_at), (blocks,), jnp.float32, least / len(cuts), largest / len(cuts))
        level = level * jnp.repeat(jnp.exp(heights), dims[axis_at] // blocks).reshape((-1,) + (1,) * (len(dims) - 1 - axis_at))
    return level


def centred(rng, extent, scale, bound, pieces=(), kind=jnp.bfloat16):
    values = jax.random.normal(rng, extent, jnp.float32) * scale
    if len(pieces) > 0:
        values = block_scale(rng, extent, pieces, -0.22, 0.18) * values
    return jnp.clip(values, min=-bound, max=bound).astype(kind)


def setup_inputs(seed: int = 0, part: int = 0) -> dict:
    arg_keys = jax.random.split(jax.random.key(seed), 14)
    part_splits = jax.random.split(jax.random.fold_in(arg_keys[13], part), 14)
    latent_old = centred(part_splits[0], (STEPS, TOKENS, C), 1.0, 6.0, ((0, 4), (1, 4)), jnp.float32)
    noise_start = centred(part_splits[1], (TOKENS, C), 1.0, 6.0, ((0, 4),), jnp.float32)
    step_index = with_ends(jax.random.randint(part_splits[2], (STEPS,), 0, TABLE - 1), jax.random.fold_in(part_splits[2], 1), 0, (TABLE - 1) - 1).astype(jnp.int32)
    sigma_table = jnp.clip(jnp.exp(jax.random.uniform(arg_keys[3], (TABLE,), jnp.float32, math.log(0.02), math.log(1.0))), 0.02, 1.0)
    mod_weight = centred(arg_keys[4], (FREQ, 3 * D), FREQ ** -0.5, 0.375)
    embed_weight = centred(arg_keys[5], (C, D), C ** -0.5, 0.75)
    embed_bias = centred(arg_keys[6], (D,), 0.5, 3.0, (), jnp.float32)
    query_weight = centred(arg_keys[7], (D, HEADS * HEAD), D ** -0.5, 0.109375, ((0, 4),))
    query_gain = jnp.clip(1.0 + 0.18 * jax.random.normal(arg_keys[8], (HEAD,), jnp.float32), 0.1, 1.9)
    stale_keys = draw_stale_keys(jax.random.fold_in(jax.random.fold_in(arg_keys[13], part), 71), part)
    stale_values = centred(part_splits[10], (STEPS, KEYS, HEADS * HEAD), 1.0, 6.0, ((0, 4), (1, 4)))
    out_weight = centred(arg_keys[11], (D, HEADS * HEAD), (HEADS * HEAD // 4) ** -0.5, 0.3125, ((0, 4),))
    final_weight = centred(arg_keys[12], (D, C), D ** -0.5, 0.109375)
    return dict(latent_old=latent_old, noise_start=noise_start, step_index=step_index, sigma_table=sigma_table, mod_weight=mod_weight, embed_weight=embed_weight, embed_bias=embed_bias, query_weight=query_weight, query_gain=query_gain, stale_keys=stale_keys, stale_values=stale_values, out_weight=out_weight, final_weight=final_weight)


epsilon = 1e-06

def layer_norm(values_in):
    row_mean = lax.optimization_barrier(jnp.mean(values_in, axis=-1, keepdims=True))
    centered = values_in - row_mean
    row_var = lax.optimization_barrier(jnp.mean(centered * centered, axis=-1, keepdims=True))
    return centered * lax.rsqrt(row_var + epsilon)

def time_embed(sigma_now):
    half_count = FREQ // 2
    frequency = jnp.exp(-math.log(10000.0) * jnp.arange(half_count).astype(jnp.float32) / half_count)
    angles = 1000.0 * sigma_now * frequency
    return jnp.concatenate([jnp.cos(angles), jnp.sin(angles)])

def reference(latent_old, noise_start, step_index, sigma_table, mod_weight, embed_weight, embed_bias, query_weight, query_gain, stale_keys, stale_values, out_weight, final_weight):

    def one_step(items):
        latent, step_slot, keys_here, values_here = items
        sigma_now = sigma_table[step_slot]
        sigma_next = sigma_table[step_slot + 1]
        embedded = jax.nn.silu(time_embed(sigma_now)).astype(jnp.bfloat16)
        modulate = jnp.dot(embedded[None, :], mod_weight, preferred_element_type=jnp.float32)[0]
        shift_vec = modulate[:D]
        scale_vec = modulate[D:2 * D]
        gate_vec = modulate[2 * D:]
        hidden = jnp.dot(latent.astype(jnp.bfloat16), embed_weight, preferred_element_type=jnp.float32) + embed_bias
        normed = (layer_norm(hidden) * (1.0 + scale_vec) + shift_vec).astype(jnp.bfloat16)
        queries = jnp.dot(normed, query_weight, preferred_element_type=jnp.float32).reshape(TOKENS, HEADS, HEAD)
        queries = queries * lax.rsqrt(lax.optimization_barrier(jnp.mean(queries * queries, axis=-1, keepdims=True)) + epsilon) * query_gain
        queries = queries.astype(jnp.bfloat16).astype(jnp.float32)
        keys_split = keys_here.reshape(KEYS, HEADS, HEAD).astype(jnp.float32)
        values_split = values_here.reshape(KEYS, HEADS, HEAD).astype(jnp.float32)
        scores = jnp.einsum('qhd,khd->hqk', queries, keys_split) / math.sqrt(HEAD)
        row_peak = lax.optimization_barrier(jnp.max(scores, axis=-1, keepdims=True))
        exp_weights = jnp.exp(scores - row_peak)
        row_total = lax.optimization_barrier(jnp.sum(exp_weights, axis=-1))
        rounded = lax.optimization_barrier(exp_weights.astype(jnp.bfloat16)).astype(jnp.float32)
        blended = jnp.einsum('hqk,khd->hqd', rounded, values_split) / row_total[..., None]
        attended = jnp.transpose(blended, (1, 0, 2)).reshape(TOKENS, HEADS * HEAD).astype(jnp.bfloat16)
        branch = jnp.dot(attended, out_weight.T, preferred_element_type=jnp.float32)
        mixed = hidden + gate_vec * branch
        velocity = jnp.dot(layer_norm(mixed).astype(jnp.bfloat16), final_weight, preferred_element_type=jnp.float32)
        return velocity * (sigma_next - sigma_now)
    terms = lax.map(one_step, (latent_old, step_index, stale_keys, stale_values))
    return noise_start[None] + jnp.cumsum(terms, axis=0)
```

```python
import functools
import math

import jax
import jax.numpy as jnp
from jax import lax
from jax.experimental import pallas as pl
from jax.experimental.pallas import tpu as pltpu
from jax.sharding import PartitionSpec as P

D = 3072
HEAD = 128
FREQ = 256
HEADS = 12


epsilon = 1e-06


def entering(shard, axis, join, neutral):
    place = lax.axis_index(axis)
    gathered = lax.all_gather(shard.astype(jnp.bfloat16), axis)
    state = jnp.zeros_like(shard) + jnp.asarray(neutral, shard.dtype)

    def one(hop, state):
        return join(state, lax.dynamic_index_in_dim(gathered, hop, 0, False).astype(shard.dtype))

    return lax.fori_loop(0, place, one, state)


def layer_norm(values_in):
    row_mean = jnp.mean(values_in, axis=-1, keepdims=True)
    centered = values_in - row_mean
    row_var = jnp.mean(centered * centered, axis=-1, keepdims=True)
    return centered * lax.rsqrt(row_var + epsilon)


def time_embed(sigma_now):
    half_count = FREQ // 2
    frequency = jnp.exp(
        -math.log(10000.0) * jnp.arange(half_count).astype(jnp.float32) / half_count
    )
    angles = 1000.0 * sigma_now * frequency
    return jnp.concatenate([jnp.cos(angles), jnp.sin(angles)])


def project_back(attended, weight_rows):
    return lax.dot_general(
        attended, weight_rows, (((1,), (1,)), ((), ())), preferred_element_type=jnp.float32
    )


def norm_queries(raw_queries, query_gain):
    token_count = raw_queries.shape[0]
    head_count = raw_queries.shape[1] // HEAD
    queries = raw_queries.reshape(token_count, head_count, HEAD)
    queries = (
        queries
        * lax.rsqrt(jnp.mean(queries * queries, axis=-1, keepdims=True) + epsilon)
        * query_gain
    )
    return queries.astype(jnp.bfloat16)


def empty_state(queries):
    token_count = queries.shape[0]
    head_count = queries.shape[1]
    return (
        jnp.full((head_count, token_count), -jnp.inf, jnp.float32),
        jnp.zeros((head_count, token_count), jnp.float32),
        jnp.zeros((head_count, token_count, HEAD), jnp.float32),
    )


def attend_block(queries, state_tuple, key_piece, value_piece):
    head_count = queries.shape[1]
    row_count = key_piece.shape[0]
    key_split = key_piece.reshape(row_count, head_count, HEAD)
    value_split = value_piece.reshape(row_count, head_count, HEAD)
    run_peak, run_total, run_sum = state_tuple
    scores = jnp.einsum(
        "qhd,khd->hqk", queries, key_split, preferred_element_type=jnp.float32
    ) / math.sqrt(HEAD)
    new_peak = jnp.max(scores, axis=-1)
    rescale = jnp.exp(run_peak - new_peak)
    exp_weights = jnp.exp(scores - new_peak[..., None])
    run_total = run_total * rescale + jnp.sum(exp_weights, axis=-1)
    run_sum = run_sum * rescale[..., None] + jnp.einsum(
        "hqk,khd->hqd",
        exp_weights.astype(jnp.bfloat16),
        value_split,
        preferred_element_type=jnp.float32,
    )
    return (new_peak, run_total, run_sum)


def finish_heads(state_tuple):
    final_peak, final_total, final_sum = state_tuple
    blended = final_sum / final_total[..., None]
    token_count = blended.shape[1]
    return jnp.transpose(blended, (1, 0, 2)).reshape(token_count, -1).astype(jnp.bfloat16)


def plain_device(
    latent_old,
    noise_start,
    step_index,
    sigma_table,
    mod_weight,
    embed_weight,
    embed_bias,
    query_weight,
    query_gain,
    stale_keys,
    stale_values,
    out_weight,
    final_weight,
):
    step_slot = step_index[0]
    table_slots = jnp.arange(sigma_table.shape[0])
    sigma_now = jnp.sum(jnp.where(table_slots == step_slot, sigma_table, 0.0))
    sigma_next = jnp.sum(jnp.where(table_slots == step_slot + 1, sigma_table, 0.0))
    embedded = jax.nn.silu(time_embed(sigma_now)).astype(jnp.bfloat16)
    modulate = jnp.dot(embedded[None, :], mod_weight, preferred_element_type=jnp.float32)[0]
    width = D
    shift_vec = modulate[:width]
    scale_vec = modulate[width : 2 * width]
    gate_vec = modulate[2 * width :]
    latent = latent_old[0]
    token_count = latent.shape[0]
    hidden = (
        jnp.dot(latent.astype(jnp.bfloat16), embed_weight, preferred_element_type=jnp.float32)
        + embed_bias
    )
    normed = (layer_norm(hidden) * (1.0 + scale_vec) + shift_vec).astype(jnp.bfloat16)
    patch_count = lax.axis_size("patch")
    group_width = HEADS // patch_count * HEAD
    patch_slot = lax.axis_index("patch")
    query_columns = lax.dynamic_slice_in_dim(query_weight, patch_slot * group_width, group_width, 1)
    normed_every = lax.all_gather(normed, "patch", axis=0, tiled=True)
    raw_every = jnp.dot(
        normed_every,
        lax.all_gather(query_columns, "step", axis=0, tiled=True),
        preferred_element_type=jnp.float32,
    )
    queries_every = norm_queries(raw_every, query_gain)
    keys_group, values_group = (
        lax.all_to_all(stale_keys[0], "patch", split_axis=1, concat_axis=0, tiled=True),
        lax.all_to_all(stale_values[0], "patch", split_axis=1, concat_axis=0, tiled=True),
    )
    state_every = attend_block(queries_every, empty_state(queries_every), keys_group, values_group)
    attended_every = finish_heads(state_every)
    attended = lax.all_to_all(attended_every, "patch", split_axis=0, concat_axis=1, tiled=True)
    branch = project_back(attended, lax.all_gather(out_weight, "step", axis=0, tiled=True))
    mixed = hidden + gate_vec * branch
    velocity = jnp.dot(
        layer_norm(mixed).astype(jnp.bfloat16), final_weight, preferred_element_type=jnp.float32
    )
    drift_term = velocity * (sigma_next - sigma_now)
    flat_term = drift_term.reshape(-1, 128)

    def add_terms(earlier, later):
        return earlier + later

    prefix = entering(flat_term, "step", add_terms, jnp.zeros_like(flat_term))
    result = noise_start + (prefix + flat_term).reshape(token_count, -1)
    return result[None]


NT = (((1,), (1,)), ((), ()))
NN = (((1,), (0,)), ((), ()))


def send(src, dst, send_sem, recv_sem, target):
    return pltpu.make_async_remote_copy(
        src_ref=src,
        dst_ref=dst,
        send_sem=send_sem,
        recv_sem=recv_sem,
        device_id=target,
        device_id_type=pl.DeviceIdType.MESH,
    )


def dot(a, b, dims=NN):
    return lax.dot_general(a, b, dims, preferred_element_type=jnp.float32)


def fused_kernel(
    sizes,
    latent_ref,
    noise_ref,
    embedded_ref,
    dt_ref,
    embed_ref,
    bias_ref,
    gain_ref,
    final_ref,
    mod_hbm,
    wq_hbm,
    key_hbm,
    value_hbm,
    wo_hbm,
    out_ref,
    lat_all,
    mod_buf,
    mod_out,
    wq_buf,
    key_buf,
    value_buf,
    wo_buf,
    normed,
    raw,
    queries,
    att,
    branch,
    embed_mine,
    bias_mine,
    gate_mine,
    final_mine,
    pay,
    pay_in,
    drift_out,
    drift_in,
    local_sem,
    lat_s,
    lat_r,
    kv_s,
    kv_r,
    wqz_s,
    wqz_r,
    wqy_s,
    wqy_r,
    woz_s,
    woz_r,
    woy_s,
    woy_r,
    att_s,
    att_r,
    pay_s,
    pay_r,
    dr_s,
    dr_r,
):
    nr, ns, np_ = sizes
    r, s, p = lax.axis_index("rep"), lax.axis_index("step"), lax.axis_index("patch")
    tokens = latent_ref.shape[0]
    total = tokens * np_
    width = embed_ref.shape[1]
    rows = wq_hbm.shape[0]
    inner = wq_hbm.shape[1]
    group = inner // np_
    heads = group // HEAD
    keys = key_hbm.shape[0]
    half = rows // nr
    mine = rows // np_
    part = mine // nr
    feats = width // np_

    def patch_of(d):
        return lax.rem(p + d, np_)

    def step_of(d):
        return lax.rem(s + d, ns)

    def rep_of(d):
        return lax.rem(r + d, nr)

    loads = [
        pltpu.make_async_copy(mod_hbm, mod_buf, local_sem.at[0]),
        pltpu.make_async_copy(
            wq_hbm.at[:, pl.ds(pl.multiple_of(p * group, HEAD), group)],
            wq_buf.at[s],
            local_sem.at[1],
        ),
        pltpu.make_async_copy(
            key_hbm.at[:, pl.ds(pl.multiple_of(p * group, HEAD), group)],
            key_buf.at[pl.ds(pl.multiple_of(p * keys, 16), keys), :],
            local_sem.at[2],
        ),
        pltpu.make_async_copy(
            value_hbm.at[:, pl.ds(pl.multiple_of(p * group, HEAD), group)],
            value_buf.at[pl.ds(pl.multiple_of(p * keys, 16), keys), :],
            local_sem.at[3],
        ),
        pltpu.make_async_copy(
            wo_hbm.at[pl.ds(pl.multiple_of(p * mine, 16), mine), :],
            wo_buf.at[pl.ds(pl.multiple_of(s * mine, 16), mine), :],
            local_sem.at[4],
        ),
    ]
    barrier = pltpu.get_barrier_semaphore()
    for d in range(1, np_):
        pl.semaphore_signal(
            barrier, inc=1, device_id={"patch": patch_of(d)}, device_id_type=pl.DeviceIdType.MESH
        )
    for d in range(1, ns):
        pl.semaphore_signal(
            barrier, inc=1, device_id={"step": step_of(d)}, device_id_type=pl.DeviceIdType.MESH
        )
    for d in range(1, nr):
        pl.semaphore_signal(
            barrier, inc=1, device_id={"rep": rep_of(d)}, device_id_type=pl.DeviceIdType.MESH
        )
    for load in loads:
        load.start()
    pl.semaphore_wait(barrier, np_ - 1 + ns - 1 + nr - 1)

    def lat_copy(d, owner):
        return send(
            latent_ref, lat_all.at[owner], lat_s.at[d], lat_r.at[d], {"patch": patch_of(d)}
        )

    def kv_copy(which, d, taker, owner):
        source = (key_hbm, value_hbm)[which]
        target = (key_buf, value_buf)[which]
        return send(
            source.at[:, pl.ds(pl.multiple_of(taker * group, HEAD), group)],
            target.at[pl.ds(pl.multiple_of(owner * keys, 16), keys), :],
            kv_s.at[which, d],
            kv_r.at[which, d],
            {"patch": taker},
        )

    def wqz_copy(d, owner):
        return send(
            wq_hbm.at[
                pl.ds(pl.multiple_of(r * half, 16), half),
                pl.ds(pl.multiple_of(p * group, HEAD), group),
            ],
            wq_buf.at[owner, pl.ds(pl.multiple_of(r * half, 16), half), :],
            wqz_s.at[d],
            wqz_r.at[d],
            {"step": step_of(d)},
        )

    def wqy_copy(d, e, from_rep):
        owner = step_of(ns - d)
        spot = wq_buf.at[owner, pl.ds(pl.multiple_of(from_rep * half, 16), half), :]
        return send(spot, spot, wqy_s.at[d, e], wqy_r.at[d, e], {"rep": rep_of(e)})

    def woz_copy(d, owner):
        return send(
            wo_hbm.at[pl.ds(pl.multiple_of(p * mine + r * part, 16), part), :],
            wo_buf.at[pl.ds(pl.multiple_of(owner * mine + r * part, 16), part), :],
            woz_s.at[d],
            woz_r.at[d],
            {"step": step_of(d)},
        )

    def woy_copy(d, e, from_rep):
        owner = step_of(ns - d)
        spot = wo_buf.at[pl.ds(pl.multiple_of(owner * mine + from_rep * part, 16), part), :]
        return send(spot, spot, woy_s.at[d, e], woy_r.at[d, e], {"rep": rep_of(e)})

    for d in range(1, np_):
        lat_copy(d, p).start()
    order = [d for d in (1, ns - 1) if d > 0] + list(range(2, ns - 1))
    order = list(dict.fromkeys(order))
    for d in order:
        wqz_copy(d, s).start()
    for which in range(2):
        for d in range(1, np_):
            kv_copy(which, d, patch_of(d), p).start()
    for d in order:
        woz_copy(d, s).start()

    loads[0].wait()
    for block in range(3):
        mod_out[:, block * width : (block + 1) * width] = dot(
            embedded_ref[...], mod_buf[:, block * width : (block + 1) * width]
        )

    for k in range(np_):

        @pl.when(p == k)
        def _():
            for z in range(ns):
                start = z * rows + k * mine
                spot = slice(z * mine, (z + 1) * mine)
                embed_mine[:, spot] = embed_ref[:, start : start + mine]
                bias_mine[:, spot] = bias_ref[:, start : start + mine]
                gate_mine[:, spot] = mod_out[
                    0:1, 2 * width + start : 2 * width + start + mine
                ]
                final_mine[spot, :] = final_ref[start : start + mine, :]

    lat_all[p] = latent_ref[...]
    for d in range(1, np_):
        lat_copy(d, patch_of(np_ - d)).wait_recv()

    small = min(128, tokens)

    def norm_block(i, _):
        at = i * small
        owner = lax.div(at, tokens)
        inside = pl.multiple_of(lax.rem(at, tokens), small)
        latent = lat_all[owner, pl.ds(inside, small), :].astype(jnp.bfloat16)
        hidden = dot(latent, embed_ref[...]) + bias_ref[...]
        centered = hidden - jnp.mean(hidden, axis=-1, keepdims=True)
        row_var = jnp.mean(centered * centered, axis=-1, keepdims=True)
        unit = centered * lax.rsqrt(row_var + epsilon)
        shifted = unit * (1.0 + mod_out[0:1, width : 2 * width]) + mod_out[0:1, 0:width]
        normed[pl.ds(pl.multiple_of(at, small), small), :] = shifted.astype(jnp.bfloat16)
        return 0

    lax.fori_loop(0, total // small, norm_block, 0)

    chunk = min(256, total)

    def project(owner, start, depth, first):
        def block(i, _):
            at = pl.ds(pl.multiple_of(i * chunk, chunk), chunk)
            lanes = pl.ds(pl.multiple_of(owner * rows + start, HEAD), depth)
            term = dot(
                normed[at, lanes],
                wq_buf[owner, pl.ds(pl.multiple_of(start, 16), depth), :],
            )
            raw[at, :] = term if first else raw[at, :] + term
            return 0

        lax.fori_loop(0, total // chunk, block, 0)

    loads[1].wait()
    project(s, 0, rows, True)
    for d in order:
        owner = step_of(ns - d)
        wqz_copy(d, owner).wait_recv()
        for e in range(1, nr):
            wqy_copy(d, e, r).start()
        project(owner, r * half, half, False)
    for d in order:
        owner = step_of(ns - d)
        for e in range(1, nr):
            other = rep_of(nr - e)
            wqy_copy(d, e, other).wait_recv()
            project(owner, other * half, half, False)

    def norm_query(i, _):
        at = pl.ds(pl.multiple_of(i * chunk, chunk), chunk)
        for h in range(heads):
            q = raw[at, h * HEAD : (h + 1) * HEAD]
            q = q * lax.rsqrt(jnp.mean(q * q, axis=-1, keepdims=True) + epsilon) * gain_ref[...]
            queries[at, h * HEAD : (h + 1) * HEAD] = q.astype(jnp.bfloat16)
        return 0

    lax.fori_loop(0, total // chunk, norm_query, 0)

    loads[2].wait()
    loads[3].wait()
    for which in range(2):
        for d in range(1, np_):
            kv_copy(which, d, p, patch_of(np_ - d)).wait_recv()

    across = lax.rem(p + 2, np_)
    beside = p + 1 - 2 * lax.rem(p, 2)
    diagonal = lax.rem(beside + 2, np_)

    def head_copy(way, h, owner):
        spot = att.at[:, pl.ds(pl.multiple_of((owner * heads + h) * HEAD, HEAD), HEAD)]
        return send(
            spot,
            spot,
            att_s.at[way, h],
            att_r.at[way, h],
            {"patch": (across if way == 0 else beside)},
        )

    def pass_on(h):
        head_copy(0, h, across).wait_recv()
        head_copy(2, h, across).start()

    factor = 1.0 / math.sqrt(HEAD)
    for h in range(heads):

        def attend(i, _):
            at = pl.ds(pl.multiple_of(i * chunk, chunk), chunk)
            lanes = slice(h * HEAD, (h + 1) * HEAD)
            scores = dot(queries[at, lanes], key_buf[:, lanes], NT)
            peak = jnp.max(scores, axis=-1, keepdims=True)
            weights = jnp.exp((scores - peak) * factor)
            row_total = jnp.sum(weights, axis=-1, keepdims=True)
            blended = dot(weights.astype(jnp.bfloat16), value_buf[:, lanes]) / row_total
            spot = pl.ds(pl.multiple_of((p * heads + h) * HEAD, HEAD), HEAD)
            att[at, spot] = blended.astype(jnp.bfloat16)
            return 0

        lax.fori_loop(0, total // chunk, attend, 0)
        head_copy(0, h, p).start()
        head_copy(1, h, p).start()
        if h >= 1:
            pass_on(h - 1)

    for d in order:
        woz_copy(d, step_of(ns - d)).wait_recv()
        for e in range(1, nr):
            woy_copy(d, e, r).start()
    for h in range(heads):
        head_copy(1, h, beside).wait_recv()
    loads[4].wait()
    for d in order:
        for e in range(1, nr):
            woy_copy(d, e, rep_of(nr - e)).wait_recv()
    pair = 2 * group
    chip = lax.div(p, 2)
    here = pl.ds(pl.multiple_of(chip * pair, HEAD), pair)
    there = pl.ds(pl.multiple_of((1 - chip) * pair, HEAD), pair)

    def near(i, _):
        at = pl.ds(pl.multiple_of(i * chunk, chunk), chunk)
        branch[at, :] = dot(att[at, here], wo_buf[:, here], NT)
        return 0

    lax.fori_loop(0, total // chunk, near, 0)
    pass_on(heads - 1)
    for h in range(heads):
        head_copy(2, h, diagonal).wait_recv()

    own_sum = jnp.sum(final_mine[...].astype(jnp.float32), axis=0, keepdims=True)
    channels = final_ref.shape[1]

    def finish(d):
        owner = patch_of(d)
        at = pl.ds(pl.multiple_of(owner * tokens, tokens), tokens)
        full = branch[at, :] + dot(att[at, there], wo_buf[:, there], NT)
        latent = lat_all[owner].astype(jnp.bfloat16)
        hidden = dot(latent, embed_mine[...]) + bias_mine[...]
        mixed = hidden + gate_mine[...] * full
        middle = jnp.mean(mixed, axis=-1, keepdims=True)
        centered = mixed - middle
        spread = jnp.sum(centered * centered, axis=-1, keepdims=True)
        lane = lax.broadcasted_iota(jnp.int32, (tokens, channels), 1)
        pay[d, :, 0:channels] = (
            dot(centered.astype(jnp.bfloat16), final_mine[...]) + middle * own_sum
        )
        pay[d, :, channels : 2 * channels] = jnp.where(lane < channels // 2, middle, spread)

    def pay_copy(d):
        return send(
            pay.at[d], pay_in.at[d], pay_s.at[d], pay_r.at[d], {"patch": patch_of(d)}
        )

    def finish_other(d, _):
        finish(d)
        pay_copy(d).start()
        return 0

    lax.fori_loop(1, np_, finish_other, 0)
    finish(0)
    for d in range(1, np_):
        pay_copy(d).wait_recv()
    every = [pay[0]] + [pay_in[d] for d in range(1, np_)]
    product = sum(item[:, 0:channels] for item in every)
    middles = [item[:, channels : channels + 1] for item in every]
    row_mean = sum(middles) / np_
    spread = sum(
        item[:, channels + channels // 2 : channels + channels // 2 + 1]
        + feats * (middle - row_mean) * (middle - row_mean)
        for item, middle in zip(every, middles)
    )
    all_sum = jnp.sum(final_ref[...].astype(jnp.float32), axis=0, keepdims=True)
    velocity = (product - row_mean * all_sum) * lax.rsqrt(spread / width + epsilon)
    drift = velocity * dt_ref[0:1, 0:1]
    drift_out[...] = drift.astype(jnp.bfloat16)

    def drift_copy(d):
        return send(
            drift_out, drift_in.at[d], dr_s.at[d], dr_r.at[d], {"step": step_of(d)}
        )

    for d in range(1, ns):

        @pl.when(s + d < ns)
        def _():
            drift_copy(d).start()

    out_ref[...] = noise_ref[...] + drift
    for d in range(1, ns):

        @pl.when(s - d >= 0)
        def _():
            drift_copy(d).wait_recv()
            out_ref[...] += drift_in[d].astype(jnp.float32)

    for d in range(1, np_):
        lat_copy(d, p).wait_send()
        pay_copy(d).wait_send()
        for which in range(2):
            kv_copy(which, d, patch_of(d), p).wait_send()
    for d in range(1, ns):
        wqz_copy(d, s).wait_send()
        woz_copy(d, s).wait_send()
        for e in range(1, nr):
            wqy_copy(d, e, r).wait_send()
            woy_copy(d, e, r).wait_send()

        @pl.when(s + d < ns)
        def _():
            drift_copy(d).wait_send()

    for h in range(heads):
        head_copy(0, h, p).wait_send()
        head_copy(1, h, p).wait_send()
        head_copy(2, h, across).wait_send()


def fused_device(
    sizes,
    latent_old,
    noise_start,
    step_index,
    sigma_table,
    mod_weight,
    embed_weight,
    embed_bias,
    query_weight,
    query_gain,
    stale_keys,
    stale_values,
    out_weight,
    final_weight,
):
    nr, ns, np_ = sizes
    step_slot = step_index[0]
    table_slots = jnp.arange(sigma_table.shape[0])
    sigma_now = jnp.sum(jnp.where(table_slots == step_slot, sigma_table, 0.0))
    sigma_next = jnp.sum(jnp.where(table_slots == step_slot + 1, sigma_table, 0.0))
    embedded = jax.nn.silu(time_embed(sigma_now)).astype(jnp.bfloat16)
    embedded = jnp.broadcast_to(embedded[None, :], (16, embedded.shape[0]))
    dt = jnp.full((1, HEAD), sigma_next - sigma_now, jnp.float32)
    tokens, channels = latent_old.shape[1:]
    width = embed_weight.shape[1]
    rows, inner = query_weight.shape
    keys = stale_keys.shape[1]
    group = inner // np_
    heads = group // HEAD
    feats = width // np_
    total = tokens * np_
    bf, f32 = jnp.bfloat16, jnp.float32
    dma = pltpu.SemaphoreType.DMA
    vmem = pl.BlockSpec(memory_space=pltpu.VMEM)
    anywhere = pl.BlockSpec(memory_space=pl.ANY)
    out = pl.pallas_call(
        functools.partial(fused_kernel, sizes),
        out_shape=jax.ShapeDtypeStruct((tokens, channels), f32),
        in_specs=[vmem] * 8 + [anywhere] * 5,
        out_specs=vmem,
        scratch_shapes=[
            pltpu.VMEM((np_, tokens, channels), f32),
            pltpu.VMEM(mod_weight.shape, bf),
            pltpu.VMEM((16, 3 * width), f32),
            pltpu.VMEM((ns, rows, group), bf),
            pltpu.VMEM((np_ * keys, group), bf),
            pltpu.VMEM((np_ * keys, group), bf),
            pltpu.VMEM((feats, inner), bf),
            pltpu.VMEM((total, width), bf),
            pltpu.VMEM((total, group), f32),
            pltpu.VMEM((total, group), bf),
            pltpu.VMEM((total, inner), bf),
            pltpu.VMEM((total, feats), f32),
            pltpu.VMEM((channels, feats), bf),
            pltpu.VMEM((1, feats), f32),
            pltpu.VMEM((1, feats), f32),
            pltpu.VMEM((feats, channels), bf),
            pltpu.VMEM((np_, tokens, 2 * channels), f32),
            pltpu.VMEM((np_, tokens, 2 * channels), f32),
            pltpu.VMEM((tokens, channels), bf),
            pltpu.VMEM((ns, tokens, channels), bf),
            dma((5,)),
            dma((np_,)),
            dma((np_,)),
            dma((2, np_)),
            dma((2, np_)),
            dma((ns,)),
            dma((ns,)),
            dma((ns, nr)),
            dma((ns, nr)),
            dma((ns,)),
            dma((ns,)),
            dma((ns, nr)),
            dma((ns, nr)),
            dma((3, heads)),
            dma((3, heads)),
            dma((np_,)),
            dma((np_,)),
            dma((ns,)),
            dma((ns,)),
        ],
        compiler_params=pltpu.CompilerParams(
            collective_id=0, has_side_effects=True, vmem_limit_bytes=60 * 1024 * 1024
        ),
    )(
        latent_old[0],
        noise_start,
        embedded,
        dt,
        embed_weight,
        embed_bias[None, :],
        query_gain[None, :],
        final_weight,
        mod_weight,
        query_weight,
        stale_keys[0],
        stale_values[0],
        out_weight,
    )
    return out[None]


def fits(mesh):
    nr, ns, np_ = (mesh.shape[axis] for axis in ("rep", "step", "patch"))
    return np_ == 4 and ns <= 8 and D % (ns * np_ * nr * 16) == 0 and D // (ns * nr) % HEAD == 0


def solution(mesh):
    placed = (
        P(("rep", "step"), "patch", None),
        P(("rep", "patch"), None),
        P(("rep", "step")),
        P(),
        P(),
        P(),
        P(),
        P("step", None),
        P(),
        P(("rep", "step"), "patch", None),
        P(("rep", "step"), "patch", None),
        P("step", None),
        P(),
    )
    sizes = tuple(mesh.shape[axis] for axis in ("rep", "step", "patch"))
    per_device = functools.partial(fused_device, sizes) if fits(mesh) else plain_device
    return jax.shard_map(
        per_device,
        mesh=mesh,
        in_specs=placed,
        out_specs=P(("rep", "step"), "patch", None),
        check_vma=False,
    )
```

```python
import functools
import math

import jax
import jax.numpy as jnp
from jax import lax
from jax.experimental import pallas as pl
from jax.experimental.pallas import tpu as pltpu
from jax.sharding import PartitionSpec as P

D = 3072
HEAD = 128
FREQ = 256
HEADS = 12


epsilon = 1e-06


def entering(shard, axis, join, neutral):
    place = lax.axis_index(axis)
    gathered = lax.all_gather(shard.astype(jnp.bfloat16), axis)
    state = jnp.zeros_like(shard) + jnp.asarray(neutral, shard.dtype)

    def one(hop, state):
        return join(state, lax.dynamic_index_in_dim(gathered, hop, 0, False).astype(shard.dtype))

    return lax.fori_loop(0, place, one, state)


def layer_norm(values_in):
    row_mean = jnp.mean(values_in, axis=-1, keepdims=True)
    centered = values_in - row_mean
    row_var = jnp.mean(centered * centered, axis=-1, keepdims=True)
    return centered * lax.rsqrt(row_var + epsilon)


def time_embed(sigma_now):
    half_count = FREQ // 2
    frequency = jnp.exp(
        -math.log(10000.0) * jnp.arange(half_count).astype(jnp.float32) / half_count
    )
    angles = 1000.0 * sigma_now * frequency
    return jnp.concatenate([jnp.cos(angles), jnp.sin(angles)])


def project_back(attended, weight_rows):
    return lax.dot_general(
        attended, weight_rows, (((1,), (1,)), ((), ())), preferred_element_type=jnp.float32
    )


def norm_queries(raw_queries, query_gain):
    token_count = raw_queries.shape[0]
    head_count = raw_queries.shape[1] // HEAD
    queries = raw_queries.reshape(token_count, head_count, HEAD)
    queries = (
        queries
        * lax.rsqrt(jnp.mean(queries * queries, axis=-1, keepdims=True) + epsilon)
        * query_gain
    )
    return queries.astype(jnp.bfloat16)


def empty_state(queries):
    token_count = queries.shape[0]
    head_count = queries.shape[1]
    return (
        jnp.full((head_count, token_count), -jnp.inf, jnp.float32),
        jnp.zeros((head_count, token_count), jnp.float32),
        jnp.zeros((head_count, token_count, HEAD), jnp.float32),
    )


def attend_block(queries, state_tuple, key_piece, value_piece):
    head_count = queries.shape[1]
    row_count = key_piece.shape[0]
    key_split = key_piece.reshape(row_count, head_count, HEAD)
    value_split = value_piece.reshape(row_count, head_count, HEAD)
    run_peak, run_total, run_sum = state_tuple
    scores = jnp.einsum(
        "qhd,khd->hqk", queries, key_split, preferred_element_type=jnp.float32
    ) / math.sqrt(HEAD)
    new_peak = jnp.max(scores, axis=-1)
    rescale = jnp.exp(run_peak - new_peak)
    exp_weights = jnp.exp(scores - new_peak[..., None])
    run_total = run_total * rescale + jnp.sum(exp_weights, axis=-1)
    run_sum = run_sum * rescale[..., None] + jnp.einsum(
        "hqk,khd->hqd",
        exp_weights.astype(jnp.bfloat16),
        value_split,
        preferred_element_type=jnp.float32,
    )
    return (new_peak, run_total, run_sum)


def finish_heads(state_tuple):
    final_peak, final_total, final_sum = state_tuple
    blended = final_sum / final_total[..., None]
    token_count = blended.shape[1]
    return jnp.transpose(blended, (1, 0, 2)).reshape(token_count, -1).astype(jnp.bfloat16)


def plain_device(
    latent_old,
    noise_start,
    step_index,
    sigma_table,
    mod_weight,
    embed_weight,
    embed_bias,
    query_weight,
    query_gain,
    stale_keys,
    stale_values,
    out_weight,
    final_weight,
):
    step_slot = step_index[0]
    table_slots = jnp.arange(sigma_table.shape[0])
    sigma_now = jnp.sum(jnp.where(table_slots == step_slot, sigma_table, 0.0))
    sigma_next = jnp.sum(jnp.where(table_slots == step_slot + 1, sigma_table, 0.0))
    embedded = jax.nn.silu(time_embed(sigma_now)).astype(jnp.bfloat16)
    modulate = jnp.dot(embedded[None, :], mod_weight, preferred_element_type=jnp.float32)[0]
    width = D
    shift_vec = modulate[:width]
    scale_vec = modulate[width : 2 * width]
    gate_vec = modulate[2 * width :]
    latent = latent_old[0]
    token_count = latent.shape[0]
    hidden = (
        jnp.dot(latent.astype(jnp.bfloat16), embed_weight, preferred_element_type=jnp.float32)
        + embed_bias
    )
    normed = (layer_norm(hidden) * (1.0 + scale_vec) + shift_vec).astype(jnp.bfloat16)
    patch_count = lax.axis_size("patch")
    group_width = HEADS // patch_count * HEAD
    patch_slot = lax.axis_index("patch")
    query_columns = lax.dynamic_slice_in_dim(query_weight, patch_slot * group_width, group_width, 1)
    normed_every = lax.all_gather(normed, "patch", axis=0, tiled=True)
    raw_every = jnp.dot(
        normed_every,
        lax.all_gather(query_columns, "step", axis=0, tiled=True),
        preferred_element_type=jnp.float32,
    )
    queries_every = norm_queries(raw_every, query_gain)
    keys_group, values_group = (
        lax.all_to_all(stale_keys[0], "patch", split_axis=1, concat_axis=0, tiled=True),
        lax.all_to_all(stale_values[0], "patch", split_axis=1, concat_axis=0, tiled=True),
    )
    state_every = attend_block(queries_every, empty_state(queries_every), keys_group, values_group)
    attended_every = finish_heads(state_every)
    attended = lax.all_to_all(attended_every, "patch", split_axis=0, concat_axis=1, tiled=True)
    branch = project_back(attended, lax.all_gather(out_weight, "step", axis=0, tiled=True))
    mixed = hidden + gate_vec * branch
    velocity = jnp.dot(
        layer_norm(mixed).astype(jnp.bfloat16), final_weight, preferred_element_type=jnp.float32
    )
    drift_term = velocity * (sigma_next - sigma_now)
    flat_term = drift_term.reshape(-1, 128)

    def add_terms(earlier, later):
        return earlier + later

    prefix = entering(flat_term, "step", add_terms, jnp.zeros_like(flat_term))
    result = noise_start + (prefix + flat_term).reshape(token_count, -1)
    return result[None]


NT = (((1,), (1,)), ((), ()))
NN = (((1,), (0,)), ((), ()))


def send(src, dst, send_sem, recv_sem, target):
    return pltpu.make_async_remote_copy(
        src_ref=src,
        dst_ref=dst,
        send_sem=send_sem,
        recv_sem=recv_sem,
        device_id=target,
        device_id_type=pl.DeviceIdType.MESH,
    )


def dot(a, b, dims=NN):
    return lax.dot_general(a, b, dims, preferred_element_type=jnp.float32)


def fused_kernel(
    sizes,
    latent_ref,
    noise_ref,
    embedded_ref,
    dt_ref,
    embed_ref,
    bias_ref,
    gain_ref,
    final_ref,
    mod_hbm,
    wq_hbm,
    key_hbm,
    value_hbm,
    wo_hbm,
    out_ref,
    lat_all,
    mod_buf,
    mod_out,
    wq_buf,
    key_buf,
    value_buf,
    wo_buf,
    normed,
    raw,
    queries,
    att,
    branch,
    embed_mine,
    bias_mine,
    gate_mine,
    final_mine,
    pay,
    pay_in,
    drift_out,
    drift_in,
    drift_sum,
    local_sem,
    lat_s,
    lat_r,
    kv_s,
    kv_r,
    wqz_s,
    wqz_r,
    wqy_s,
    wqy_r,
    woz_s,
    woz_r,
    woy_s,
    woy_r,
    att_s,
    att_r,
    pay_s,
    pay_r,
    dr_s,
    dr_r,
):
    nr, ns, np_ = sizes
    r, s, p = lax.axis_index("rep"), lax.axis_index("step"), lax.axis_index("patch")
    channels, tokens = latent_ref.shape
    total = tokens * np_
    width = embed_ref.shape[1]
    rows = wq_hbm.shape[0]
    inner = wq_hbm.shape[1]
    group = inner // np_
    heads = group // HEAD
    keys = key_hbm.shape[0]
    half = rows // nr
    mine = rows // np_
    part = mine // nr
    feats = width // np_

    def patch_of(d):
        return lax.rem(p + d, np_)

    def step_of(d):
        return lax.rem(s + d, ns)

    def rep_of(d):
        return lax.rem(r + d, nr)

    loads = [
        pltpu.make_async_copy(mod_hbm, mod_buf, local_sem.at[0]),
        pltpu.make_async_copy(
            wq_hbm.at[:, pl.ds(pl.multiple_of(p * group, HEAD), group)],
            wq_buf.at[s],
            local_sem.at[1],
        ),
        pltpu.make_async_copy(
            key_hbm.at[:, pl.ds(pl.multiple_of(p * group, HEAD), group)],
            key_buf.at[pl.ds(pl.multiple_of(p * keys, 16), keys), :],
            local_sem.at[2],
        ),
        pltpu.make_async_copy(
            value_hbm.at[:, pl.ds(pl.multiple_of(p * group, HEAD), group)],
            value_buf.at[pl.ds(pl.multiple_of(p * keys, 16), keys), :],
            local_sem.at[3],
        ),
        pltpu.make_async_copy(
            wo_hbm.at[pl.ds(pl.multiple_of(p * mine, 16), mine), :],
            wo_buf.at[pl.ds(pl.multiple_of(s * mine, 16), mine), :],
            local_sem.at[4],
        ),
    ]
    barrier = pltpu.get_barrier_semaphore()
    for d in range(1, np_):
        pl.semaphore_signal(
            barrier, inc=1, device_id={"patch": patch_of(d)}, device_id_type=pl.DeviceIdType.MESH
        )
    for d in range(1, ns):
        pl.semaphore_signal(
            barrier, inc=1, device_id={"step": step_of(d)}, device_id_type=pl.DeviceIdType.MESH
        )
    for d in range(1, nr):
        pl.semaphore_signal(
            barrier, inc=1, device_id={"rep": rep_of(d)}, device_id_type=pl.DeviceIdType.MESH
        )
    for load in loads:
        load.start()
    pl.semaphore_wait(barrier, np_ - 1 + ns - 1 + nr - 1)

    def lat_copy(d, owner):
        return send(
            latent_ref, lat_all.at[owner], lat_s.at[d], lat_r.at[d], {"patch": patch_of(d)}
        )

    def kv_copy(which, d, taker, owner):
        source = (key_hbm, value_hbm)[which]
        target = (key_buf, value_buf)[which]
        return send(
            source.at[:, pl.ds(pl.multiple_of(taker * group, HEAD), group)],
            target.at[pl.ds(pl.multiple_of(owner * keys, 16), keys), :],
            kv_s.at[which, d],
            kv_r.at[which, d],
            {"patch": taker},
        )

    def wqz_copy(d, owner):
        return send(
            wq_hbm.at[
                pl.ds(pl.multiple_of(r * half, 16), half),
                pl.ds(pl.multiple_of(p * group, HEAD), group),
            ],
            wq_buf.at[owner, pl.ds(pl.multiple_of(r * half, 16), half), :],
            wqz_s.at[d],
            wqz_r.at[d],
            {"step": step_of(d)},
        )

    def wqy_copy(d, e, from_rep):
        owner = step_of(ns - d)
        spot = wq_buf.at[owner, pl.ds(pl.multiple_of(from_rep * half, 16), half), :]
        return send(spot, spot, wqy_s.at[d, e], wqy_r.at[d, e], {"rep": rep_of(e)})

    def woz_copy(d, owner):
        return send(
            wo_hbm.at[pl.ds(pl.multiple_of(p * mine + r * part, 16), part), :],
            wo_buf.at[pl.ds(pl.multiple_of(owner * mine + r * part, 16), part), :],
            woz_s.at[d],
            woz_r.at[d],
            {"step": step_of(d)},
        )

    def woy_copy(d, e, from_rep):
        owner = step_of(ns - d)
        spot = wo_buf.at[pl.ds(pl.multiple_of(owner * mine + from_rep * part, 16), part), :]
        return send(spot, spot, woy_s.at[d, e], woy_r.at[d, e], {"rep": rep_of(e)})

    for d in range(1, np_):
        lat_copy(d, p).start()
    relayed = ns == 4
    if relayed:
        early = 3 - 2 * jnp.minimum(s, 1)
        order = [2, early, 4 - early]
    else:
        order = list(range(1, ns))

    def start_direct(copy):
        for d in [2, 1, 3] if relayed else order:
            if relayed and d != 2:

                @pl.when(s != (0 if d == 3 else ns - 1))
                def _():
                    copy(d, s).start()

            else:
                copy(d, s).start()

    def direct_sent(copy):
        for d in range(1, ns):
            if relayed and d != 2:

                @pl.when(s != (0 if d == 3 else ns - 1))
                def _():
                    copy(d, s).wait_send()

            else:
                copy(d, s).wait_send()

    def relay(spot, send_sem, recv_sem, act):
        if relayed:
            for place, target, d in ((2, 3, 3), (1, 0, 1)):

                @pl.when(s == place)
                def _():
                    act(send(spot, spot, send_sem.at[0], recv_sem.at[d], {"step": target}))

    def wq_relay(act):
        spot = wq_buf.at[step_of(ns - 2), pl.ds(pl.multiple_of(r * half, 16), half), :]
        relay(spot, wqz_s, wqz_r, act)

    def wo_relay(act):
        at = pl.multiple_of(step_of(ns - 2) * mine + r * part, 16)
        relay(wo_buf.at[pl.ds(at, part), :], woz_s, woz_r, act)

    start_direct(wqz_copy)
    for which in range(2):
        for d in range(1, np_):
            kv_copy(which, d, patch_of(d), p).start()
    loads[0].wait()
    for block in range(3):
        mod_out[:, block * width : (block + 1) * width] = dot(
            embedded_ref[...], mod_buf[:, block * width : (block + 1) * width]
        )

    for k in range(np_):

        @pl.when(p == k)
        def _():
            for z in range(ns):
                start = z * rows + k * mine
                spot = slice(z * mine, (z + 1) * mine)
                embed_mine[:, spot] = embed_ref[:, start : start + mine]
                bias_mine[:, spot] = bias_ref[:, start : start + mine]
                gate_mine[:, spot] = mod_out[
                    0:1, 2 * width + start : 2 * width + start + mine
                ]
                final_mine[:, spot] = final_ref[:, start : start + mine]

    lat_all[p] = latent_ref[...]
    for d in range(1, np_):
        lat_copy(d, patch_of(np_ - d)).wait_recv()

    small = min(128, tokens)

    def norm_block(i, _):
        at = i * small
        owner = lax.div(at, tokens)
        inside = pl.multiple_of(lax.rem(at, tokens), small)
        latent = lat_all[owner, :, pl.ds(inside, small)].T.astype(jnp.bfloat16)
        hidden = dot(latent, embed_ref[...]) + bias_ref[...]
        centered = hidden - jnp.mean(hidden, axis=-1, keepdims=True)
        row_var = jnp.mean(centered * centered, axis=-1, keepdims=True)
        unit = centered * lax.rsqrt(row_var + epsilon)
        shifted = unit * (1.0 + mod_out[0:1, width : 2 * width]) + mod_out[0:1, 0:width]
        normed[pl.ds(pl.multiple_of(at, small), small), :] = shifted.astype(jnp.bfloat16)
        return 0

    lax.fori_loop(0, total // small, norm_block, 0)

    chunk = min(256, total)

    def project(owner, start, depth, first):
        def block(i, _):
            at = pl.ds(pl.multiple_of(i * chunk, chunk), chunk)
            lanes = pl.ds(pl.multiple_of(owner * rows + start, HEAD), depth)
            term = dot(
                normed[at, lanes],
                wq_buf[owner, pl.ds(pl.multiple_of(start, 16), depth), :],
            )
            raw[at, :] = term if first else raw[at, :] + term
            return 0

        lax.fori_loop(0, total // chunk, block, 0)

    loads[1].wait()
    project(s, 0, rows, True)
    for d in order:
        owner = step_of(ns - d)
        wqz_copy(d, owner).wait_recv()
        if d is order[0]:
            wq_relay(lambda copy: copy.start())
            start_direct(woz_copy)
        for e in range(1, nr):
            wqy_copy(d, e, r).start()
        project(owner, r * half, half, False)
    for d in order:
        owner = step_of(ns - d)
        for e in range(1, nr):
            other = rep_of(nr - e)
            wqy_copy(d, e, other).wait_recv()
            project(owner, other * half, half, False)

    def norm_query(i, _):
        at = pl.ds(pl.multiple_of(i * chunk, chunk), chunk)
        for h in range(heads):
            q = raw[at, h * HEAD : (h + 1) * HEAD]
            q = q * lax.rsqrt(jnp.mean(q * q, axis=-1, keepdims=True) + epsilon) * gain_ref[...]
            queries[at, h * HEAD : (h + 1) * HEAD] = q.astype(jnp.bfloat16)
        return 0

    lax.fori_loop(0, total // chunk, norm_query, 0)

    loads[2].wait()
    loads[3].wait()
    for which in range(2):
        for d in range(1, np_):
            kv_copy(which, d, p, patch_of(np_ - d)).wait_recv()

    across = lax.rem(p + 2, np_)
    beside = p + 1 - 2 * lax.rem(p, 2)
    diagonal = lax.rem(beside + 2, np_)

    def head_copy(way, h, owner):
        spot = att.at[:, pl.ds(pl.multiple_of((owner * heads + h) * HEAD, HEAD), HEAD)]
        return send(
            spot,
            spot,
            att_s.at[way, h],
            att_r.at[way, h],
            {"patch": (across if way == 0 else beside)},
        )

    def pass_on(h):
        head_copy(0, h, across).wait_recv()
        head_copy(2, h, across).start()

    def wo_pass(d):
        woz_copy(d, step_of(ns - d)).wait_recv()
        if d is order[0]:
            wo_relay(lambda copy: copy.start())
        for e in range(1, nr):
            woy_copy(d, e, r).start()

    factor = 1.0 / math.sqrt(HEAD)
    for h in range(heads):

        def attend(i, _):
            at = pl.ds(pl.multiple_of(i * chunk, chunk), chunk)
            lanes = slice(h * HEAD, (h + 1) * HEAD)
            scores = dot(queries[at, lanes], key_buf[:, lanes], NT)
            peak = jnp.max(scores, axis=-1, keepdims=True)
            weights = jnp.exp((scores - peak) * factor)
            row_total = jnp.sum(weights, axis=-1, keepdims=True)
            blended = dot(weights.astype(jnp.bfloat16), value_buf[:, lanes]) / row_total
            spot = pl.ds(pl.multiple_of((p * heads + h) * HEAD, HEAD), HEAD)
            att[at, spot] = blended.astype(jnp.bfloat16)
            return 0

        lax.fori_loop(0, total // chunk, attend, 0)
        head_copy(0, h, p).start()
        head_copy(1, h, p).start()
        if h >= 1:
            pass_on(h - 1)
        if h == heads - 2:
            wo_pass(order[0])

    for d in order[1:]:
        wo_pass(d)
    pass_on(heads - 1)
    for h in range(heads):
        head_copy(1, h, beside).wait_recv()
    loads[4].wait()
    for d in order:
        for e in range(1, nr):
            woy_copy(d, e, rep_of(nr - e)).wait_recv()
    pair = 2 * group
    chip = lax.div(p, 2)
    here = pl.ds(pl.multiple_of(chip * pair, HEAD), pair)
    there = pl.ds(pl.multiple_of((1 - chip) * pair, HEAD), pair)

    def near(i, _):
        at = pl.ds(pl.multiple_of(i * chunk, chunk), chunk)
        branch[at, :] = dot(att[at, here], wo_buf[:, here], NT)
        return 0

    lax.fori_loop(0, total // chunk, near, 0)
    for h in range(heads):
        head_copy(2, h, diagonal).wait_recv()

    own_sum = dot(jnp.ones((16, feats), jnp.bfloat16), final_mine[...], NT)[0:1]

    def partner(d):
        return jnp.where(d == 1, across, jnp.where(d == 2, diagonal, jnp.where(d == 3, beside, p)))

    def finish(d):
        owner = partner(d)
        at = pl.ds(pl.multiple_of(owner * tokens, tokens), tokens)
        full = branch[at, :] + dot(att[at, there], wo_buf[:, there], NT)
        latent = lat_all[owner].T.astype(jnp.bfloat16)
        hidden = dot(latent, embed_mine[...]) + bias_mine[...]
        mixed = hidden + gate_mine[...] * full
        middle = jnp.mean(mixed, axis=-1, keepdims=True)
        centered = mixed - middle
        spread = jnp.sum(centered * centered, axis=-1, keepdims=True)
        lane = lax.broadcasted_iota(jnp.int32, (tokens, channels), 1)
        pay[d, :, 0:channels] = (
            dot(centered.astype(jnp.bfloat16), final_mine[...], NT) + middle * own_sum
        )
        pay[d, :, channels : 2 * channels] = jnp.where(lane < channels // 2, middle, spread)

    def pay_copy(d):
        return send(
            pay.at[d], pay_in.at[d], pay_s.at[d], pay_r.at[d], {"patch": partner(d)}
        )

    def finish_other(d, _):
        finish(d)
        pay_copy(d).start()
        return 0

    lax.fori_loop(1, np_, finish_other, 0)
    finish(0)
    for d in range(1, np_):
        pay_copy(d).wait_recv()
    every = [pay[0]] + [pay_in[d] for d in range(1, np_)]
    product = sum(item[:, 0:channels] for item in every)
    middles = [item[:, channels : channels + 1] for item in every]
    row_mean = sum(middles) / np_
    spread = sum(
        item[:, channels + channels // 2 : channels + channels // 2 + 1]
        + feats * (middle - row_mean) * (middle - row_mean)
        for item, middle in zip(every, middles)
    )
    all_sum = dot(jnp.ones((16, width), jnp.bfloat16), final_ref[...], NT)[0:1]
    velocity = (product - row_mean * all_sum) * lax.rsqrt(spread / width + epsilon)
    drift = velocity * dt_ref[0:1, 0:1]
    drift_out[...] = drift.astype(jnp.bfloat16)

    def drift_copy(d):
        return send(
            drift_out, drift_in.at[d], dr_s.at[d], dr_r.at[d], {"step": step_of(d)}
        )

    for d in range(1, ns):

        @pl.when(s + d < ns)
        def _():
            drift_copy(d).start()

    drift_sum[...] = drift
    for d in range(1, ns):

        @pl.when(s - d >= 0)
        def _():
            drift_copy(d).wait_recv()
            drift_sum[...] += drift_in[d].astype(jnp.float32)

    out_ref[...] = noise_ref[...] + drift_sum[...].T

    for d in range(1, np_):
        lat_copy(d, p).wait_send()
        pay_copy(d).wait_send()
        for which in range(2):
            kv_copy(which, d, patch_of(d), p).wait_send()
    direct_sent(wqz_copy)
    direct_sent(woz_copy)
    wq_relay(lambda copy: copy.wait_send())
    wo_relay(lambda copy: copy.wait_send())
    for d in range(1, ns):
        for e in range(1, nr):
            wqy_copy(d, e, r).wait_send()
            woy_copy(d, e, r).wait_send()

        @pl.when(s + d < ns)
        def _():
            drift_copy(d).wait_send()

    for h in range(heads):
        head_copy(0, h, p).wait_send()
        head_copy(1, h, p).wait_send()
        head_copy(2, h, across).wait_send()


def fused_device(
    sizes,
    latent_old,
    noise_start,
    step_index,
    sigma_table,
    mod_weight,
    embed_weight,
    embed_bias,
    query_weight,
    query_gain,
    stale_keys,
    stale_values,
    out_weight,
    final_weight,
):
    nr, ns, np_ = sizes
    step_slot = step_index[0]
    table_slots = jnp.arange(sigma_table.shape[0])
    sigma_now = jnp.sum(jnp.where(table_slots == step_slot, sigma_table, 0.0))
    sigma_next = jnp.sum(jnp.where(table_slots == step_slot + 1, sigma_table, 0.0))
    embedded = jax.nn.silu(time_embed(sigma_now)).astype(jnp.bfloat16)
    embedded = jnp.broadcast_to(embedded[None, :], (16, embedded.shape[0]))
    dt = jnp.full((1, HEAD), sigma_next - sigma_now, jnp.float32)
    tokens, channels = latent_old.shape[1:]
    width = embed_weight.shape[1]
    rows, inner = query_weight.shape
    keys = stale_keys.shape[1]
    group = inner // np_
    heads = group // HEAD
    feats = width // np_
    total = tokens * np_
    bf, f32 = jnp.bfloat16, jnp.float32
    dma = pltpu.SemaphoreType.DMA
    vmem = pl.BlockSpec(memory_space=pltpu.VMEM)
    anywhere = pl.BlockSpec(memory_space=pl.ANY)
    out = pl.pallas_call(
        functools.partial(fused_kernel, sizes),
        out_shape=jax.ShapeDtypeStruct((channels, tokens), f32),
        in_specs=[vmem] * 8 + [anywhere] * 5,
        out_specs=vmem,
        scratch_shapes=[
            pltpu.VMEM((np_, channels, tokens), f32),
            pltpu.VMEM(mod_weight.shape, bf),
            pltpu.VMEM((16, 3 * width), f32),
            pltpu.VMEM((ns, rows, group), bf),
            pltpu.VMEM((np_ * keys, group), bf),
            pltpu.VMEM((np_ * keys, group), bf),
            pltpu.VMEM((feats, inner), bf),
            pltpu.VMEM((total, width), bf),
            pltpu.VMEM((total, group), f32),
            pltpu.VMEM((total, group), bf),
            pltpu.VMEM((total, inner), bf),
            pltpu.VMEM((total, feats), f32),
            pltpu.VMEM((channels, feats), bf),
            pltpu.VMEM((1, feats), f32),
            pltpu.VMEM((1, feats), f32),
            pltpu.VMEM((channels, feats), bf),
            pltpu.VMEM((np_, tokens, 2 * channels), f32),
            pltpu.VMEM((np_, tokens, 2 * channels), f32),
            pltpu.VMEM((tokens, channels), bf),
            pltpu.VMEM((ns, tokens, channels), bf),
            pltpu.VMEM((tokens, channels), f32),
            dma((5,)),
            dma((np_,)),
            dma((np_,)),
            dma((2, np_)),
            dma((2, np_)),
            dma((ns,)),
            dma((ns,)),
            dma((ns, nr)),
            dma((ns, nr)),
            dma((ns,)),
            dma((ns,)),
            dma((ns, nr)),
            dma((ns, nr)),
            dma((3, heads)),
            dma((3, heads)),
            dma((np_,)),
            dma((np_,)),
            dma((ns,)),
            dma((ns,)),
        ],
        compiler_params=pltpu.CompilerParams(
            collective_id=0, has_side_effects=True, vmem_limit_bytes=60 * 1024 * 1024
        ),
    )(
        latent_old[0].T,
        noise_start.T,
        embedded,
        dt,
        embed_weight,
        embed_bias[None, :],
        query_gain[None, :],
        final_weight.T,
        mod_weight,
        query_weight,
        stale_keys[0],
        stale_values[0],
        out_weight,
    )
    return out.T[None]


def fits(mesh):
    nr, ns, np_ = (mesh.shape[axis] for axis in ("rep", "step", "patch"))
    return np_ == 4 and ns <= 4 and D % (ns * np_ * nr * 16) == 0 and D // (ns * nr) % HEAD == 0


def solution(mesh):
    placed = (
        P(("rep", "step"), "patch", None),
        P(("rep", "patch"), None),
        P(("rep", "step")),
        P(),
        P(),
        P(),
        P(),
        P("step", None),
        P(),
        P(("rep", "step"), "patch", None),
        P(("rep", "step"), "patch", None),
        P("step", None),
        P(),
    )
    sizes = tuple(mesh.shape[axis] for axis in ("rep", "step", "patch"))
    per_device = functools.partial(fused_device, sizes) if fits(mesh) else plain_device
    return jax.shard_map(
        per_device,
        mesh=mesh,
        in_specs=placed,
        out_specs=P(("rep", "step"), "patch", None),
        check_vma=False,
    )
```

```python
import functools
import math

import jax
import jax.numpy as jnp
from jax import lax
from jax.experimental import pallas as pl
from jax.experimental.pallas import tpu as pltpu
from jax.sharding import PartitionSpec as P

D = 3072
HEAD = 128
FREQ = 256
HEADS = 12


epsilon = 1e-06
CUTS = 2


def entering(shard, axis, join, neutral):
    place = lax.axis_index(axis)
    gathered = lax.all_gather(shard.astype(jnp.bfloat16), axis)
    state = jnp.zeros_like(shard) + jnp.asarray(neutral, shard.dtype)

    def one(hop, state):
        return join(state, lax.dynamic_index_in_dim(gathered, hop, 0, False).astype(shard.dtype))

    return lax.fori_loop(0, place, one, state)


def layer_norm(values_in):
    row_mean = jnp.mean(values_in, axis=-1, keepdims=True)
    centered = values_in - row_mean
    row_var = jnp.mean(centered * centered, axis=-1, keepdims=True)
    return centered * lax.rsqrt(row_var + epsilon)


def time_embed(sigma_now):
    half_count = FREQ // 2
    frequency = jnp.exp(
        -math.log(10000.0) * jnp.arange(half_count).astype(jnp.float32) / half_count
    )
    angles = 1000.0 * sigma_now * frequency
    return jnp.concatenate([jnp.cos(angles), jnp.sin(angles)])


def project_back(attended, weight_rows):
    return lax.dot_general(
        attended, weight_rows, (((1,), (1,)), ((), ())), preferred_element_type=jnp.float32
    )


def norm_queries(raw_queries, query_gain):
    token_count = raw_queries.shape[0]
    head_count = raw_queries.shape[1] // HEAD
    queries = raw_queries.reshape(token_count, head_count, HEAD)
    queries = (
        queries
        * lax.rsqrt(jnp.mean(queries * queries, axis=-1, keepdims=True) + epsilon)
        * query_gain
    )
    return queries.astype(jnp.bfloat16)


def empty_state(queries):
    token_count = queries.shape[0]
    head_count = queries.shape[1]
    return (
        jnp.full((head_count, token_count), -jnp.inf, jnp.float32),
        jnp.zeros((head_count, token_count), jnp.float32),
        jnp.zeros((head_count, token_count, HEAD), jnp.float32),
    )


def attend_block(queries, state_tuple, key_piece, value_piece):
    head_count = queries.shape[1]
    row_count = key_piece.shape[0]
    key_split = key_piece.reshape(row_count, head_count, HEAD)
    value_split = value_piece.reshape(row_count, head_count, HEAD)
    run_peak, run_total, run_sum = state_tuple
    scores = jnp.einsum(
        "qhd,khd->hqk", queries, key_split, preferred_element_type=jnp.float32
    ) / math.sqrt(HEAD)
    new_peak = jnp.max(scores, axis=-1)
    rescale = jnp.exp(run_peak - new_peak)
    exp_weights = jnp.exp(scores - new_peak[..., None])
    run_total = run_total * rescale + jnp.sum(exp_weights, axis=-1)
    run_sum = run_sum * rescale[..., None] + jnp.einsum(
        "hqk,khd->hqd",
        exp_weights.astype(jnp.bfloat16),
        value_split,
        preferred_element_type=jnp.float32,
    )
    return (new_peak, run_total, run_sum)


def finish_heads(state_tuple):
    final_peak, final_total, final_sum = state_tuple
    blended = final_sum / final_total[..., None]
    token_count = blended.shape[1]
    return jnp.transpose(blended, (1, 0, 2)).reshape(token_count, -1).astype(jnp.bfloat16)


def plain_device(
    latent_old,
    noise_start,
    step_index,
    sigma_table,
    mod_weight,
    embed_weight,
    embed_bias,
    query_weight,
    query_gain,
    stale_keys,
    stale_values,
    out_weight,
    final_weight,
):
    step_slot = step_index[0]
    table_slots = jnp.arange(sigma_table.shape[0])
    sigma_now = jnp.sum(jnp.where(table_slots == step_slot, sigma_table, 0.0))
    sigma_next = jnp.sum(jnp.where(table_slots == step_slot + 1, sigma_table, 0.0))
    embedded = jax.nn.silu(time_embed(sigma_now)).astype(jnp.bfloat16)
    modulate = jnp.dot(embedded[None, :], mod_weight, preferred_element_type=jnp.float32)[0]
    width = D
    shift_vec = modulate[:width]
    scale_vec = modulate[width : 2 * width]
    gate_vec = modulate[2 * width :]
    latent = latent_old[0]
    token_count = latent.shape[0]
    hidden = (
        jnp.dot(latent.astype(jnp.bfloat16), embed_weight, preferred_element_type=jnp.float32)
        + embed_bias
    )
    normed = (layer_norm(hidden) * (1.0 + scale_vec) + shift_vec).astype(jnp.bfloat16)
    patch_count = lax.axis_size("patch")
    group_width = HEADS // patch_count * HEAD
    patch_slot = lax.axis_index("patch")
    query_columns = lax.dynamic_slice_in_dim(query_weight, patch_slot * group_width, group_width, 1)
    normed_every = lax.all_gather(normed, "patch", axis=0, tiled=True)
    raw_every = jnp.dot(
        normed_every,
        lax.all_gather(query_columns, "step", axis=0, tiled=True),
        preferred_element_type=jnp.float32,
    )
    queries_every = norm_queries(raw_every, query_gain)
    keys_group, values_group = (
        lax.all_to_all(stale_keys[0], "patch", split_axis=1, concat_axis=0, tiled=True),
        lax.all_to_all(stale_values[0], "patch", split_axis=1, concat_axis=0, tiled=True),
    )
    state_every = attend_block(queries_every, empty_state(queries_every), keys_group, values_group)
    attended_every = finish_heads(state_every)
    attended = lax.all_to_all(attended_every, "patch", split_axis=0, concat_axis=1, tiled=True)
    branch = project_back(attended, lax.all_gather(out_weight, "step", axis=0, tiled=True))
    mixed = hidden + gate_vec * branch
    velocity = jnp.dot(
        layer_norm(mixed).astype(jnp.bfloat16), final_weight, preferred_element_type=jnp.float32
    )
    drift_term = velocity * (sigma_next - sigma_now)
    flat_term = drift_term.reshape(-1, 128)

    def add_terms(earlier, later):
        return earlier + later

    prefix = entering(flat_term, "step", add_terms, jnp.zeros_like(flat_term))
    result = noise_start + (prefix + flat_term).reshape(token_count, -1)
    return result[None]


NT = (((1,), (1,)), ((), ()))
NN = (((1,), (0,)), ((), ()))


def send(src, dst, send_sem, recv_sem, target):
    return pltpu.make_async_remote_copy(
        src_ref=src,
        dst_ref=dst,
        send_sem=send_sem,
        recv_sem=recv_sem,
        device_id=target,
        device_id_type=pl.DeviceIdType.MESH,
    )


def dot(a, b, dims=NN):
    return lax.dot_general(a, b, dims, preferred_element_type=jnp.float32)


def fused_kernel(
    sizes,
    latent_ref,
    noise_ref,
    embedded_ref,
    dt_ref,
    embed_ref,
    bias_ref,
    gain_ref,
    final_ref,
    mod_hbm,
    wq_hbm,
    key_hbm,
    value_hbm,
    wo_hbm,
    out_ref,
    lat_all,
    mod_buf,
    mod_out,
    wq_buf,
    key_buf,
    value_buf,
    wo_buf,
    normed,
    raw,
    queries,
    att,
    branch,
    embed_mine,
    bias_mine,
    gate_mine,
    final_mine,
    pay,
    pay_in,
    drift_out,
    drift_in,
    drift_sum,
    local_sem,
    lat_s,
    lat_r,
    kv_s,
    kv_r,
    wqz_s,
    wqz_r,
    wqy_s,
    wqy_r,
    woz_s,
    woz_r,
    woy_s,
    woy_r,
    att_s,
    att_r,
    pay_s,
    pay_r,
    dr_s,
    dr_r,
):
    nr, ns, np_ = sizes
    r, s, p = lax.axis_index("rep"), lax.axis_index("step"), lax.axis_index("patch")
    channels, tokens = latent_ref.shape
    total = tokens * np_
    width = embed_ref.shape[1]
    rows = wq_hbm.shape[0]
    inner = wq_hbm.shape[1]
    group = inner // np_
    heads = group // HEAD
    keys = key_hbm.shape[0]
    half = rows // nr
    mine = rows // np_
    part = mine // nr
    feats = width // np_
    cuts = CUTS
    half_cut = half // cuts
    part_cut = part // cuts

    def patch_of(d):
        return lax.rem(p + d, np_)

    def step_of(d):
        return lax.rem(s + d, ns)

    def rep_of(d):
        return lax.rem(r + d, nr)

    loads = [
        pltpu.make_async_copy(mod_hbm, mod_buf, local_sem.at[0]),
        pltpu.make_async_copy(
            wq_hbm.at[:, pl.ds(pl.multiple_of(p * group, HEAD), group)],
            wq_buf.at[s],
            local_sem.at[1],
        ),
        pltpu.make_async_copy(
            key_hbm.at[:, pl.ds(pl.multiple_of(p * group, HEAD), group)],
            key_buf.at[pl.ds(pl.multiple_of(p * keys, 16), keys), :],
            local_sem.at[2],
        ),
        pltpu.make_async_copy(
            value_hbm.at[:, pl.ds(pl.multiple_of(p * group, HEAD), group)],
            value_buf.at[pl.ds(pl.multiple_of(p * keys, 16), keys), :],
            local_sem.at[3],
        ),
        pltpu.make_async_copy(
            wo_hbm.at[pl.ds(pl.multiple_of(p * mine, 16), mine), :],
            wo_buf.at[pl.ds(pl.multiple_of(s * mine, 16), mine), :],
            local_sem.at[4],
        ),
    ]
    barrier = pltpu.get_barrier_semaphore()
    for d in range(1, np_):
        pl.semaphore_signal(
            barrier, inc=1, device_id={"patch": patch_of(d)}, device_id_type=pl.DeviceIdType.MESH
        )
    for d in range(1, ns):
        pl.semaphore_signal(
            barrier, inc=1, device_id={"step": step_of(d)}, device_id_type=pl.DeviceIdType.MESH
        )
    for d in range(1, nr):
        pl.semaphore_signal(
            barrier, inc=1, device_id={"rep": rep_of(d)}, device_id_type=pl.DeviceIdType.MESH
        )
    for load in loads:
        load.start()
    pl.semaphore_wait(barrier, np_ - 1 + ns - 1 + nr - 1)

    def lat_copy(d, owner):
        return send(
            latent_ref, lat_all.at[owner], lat_s.at[d], lat_r.at[d], {"patch": patch_of(d)}
        )

    def kv_copy(which, d, taker, owner):
        source = (key_hbm, value_hbm)[which]
        target = (key_buf, value_buf)[which]
        return send(
            source.at[:, pl.ds(pl.multiple_of(taker * group, HEAD), group)],
            target.at[pl.ds(pl.multiple_of(owner * keys, 16), keys), :],
            kv_s.at[which, d],
            kv_r.at[which, d],
            {"patch": taker},
        )

    def wq_rows(from_rep, c):
        return pl.ds(pl.multiple_of(from_rep * half + c * half_cut, 16), half_cut)

    def wo_rows(base, from_rep, c):
        return pl.ds(pl.multiple_of(base * mine + from_rep * part + c * part_cut, 16), part_cut)

    def wqz_copy(d, owner, c):
        return send(
            wq_hbm.at[wq_rows(r, c), pl.ds(pl.multiple_of(p * group, HEAD), group)],
            wq_buf.at[owner, wq_rows(r, c), :],
            wqz_s.at[d, c],
            wqz_r.at[d, c],
            {"step": step_of(d)},
        )

    def wqy_copy(d, e, from_rep, c):
        spot = wq_buf.at[step_of(ns - d), wq_rows(from_rep, c), :]
        return send(spot, spot, wqy_s.at[d, e, c], wqy_r.at[d, e, c], {"rep": rep_of(e)})

    def woz_copy(d, owner, c):
        return send(
            wo_hbm.at[wo_rows(p, r, c), :],
            wo_buf.at[wo_rows(owner, r, c), :],
            woz_s.at[d, c],
            woz_r.at[d, c],
            {"step": step_of(d)},
        )

    def woy_copy(d, e, from_rep, c):
        spot = wo_buf.at[wo_rows(step_of(ns - d), from_rep, c), :]
        return send(spot, spot, woy_s.at[d, e, c], woy_r.at[d, e, c], {"rep": rep_of(e)})

    for d in range(1, np_):
        lat_copy(d, p).start()
    relayed = ns == 4
    if relayed:
        early = 3 - 2 * jnp.minimum(s, 1)
        order = [2, early, 4 - early]
    else:
        order = list(range(1, ns))

    def each_direct(copy, act):
        for d in [2, 1, 3] if relayed else order:
            for c in range(cuts):
                if relayed and d != 2:

                    @pl.when(s != (0 if d == 3 else ns - 1))
                    def _():
                        act(copy(d, s, c))

                else:
                    act(copy(d, s, c))

    def relay(spot, send_sem, recv_sem, c, act):
        if relayed:
            for place, target, d in ((2, 3, 3), (1, 0, 1)):

                @pl.when(s == place)
                def _():
                    act(send(spot, spot, send_sem.at[0, c], recv_sem.at[d, c], {"step": target}))

    def wq_relay(c, act):
        relay(wq_buf.at[step_of(ns - 2), wq_rows(r, c), :], wqz_s, wqz_r, c, act)

    def wo_relay(c, act):
        relay(wo_buf.at[wo_rows(step_of(ns - 2), r, c), :], woz_s, woz_r, c, act)

    def begin(copy):
        copy.start()

    def sent(copy):
        copy.wait_send()

    each_direct(wqz_copy, begin)
    for which in range(2):
        for d in range(1, np_):
            kv_copy(which, d, patch_of(d), p).start()
    loads[0].wait()
    embedded = jnp.broadcast_to(embedded_ref[...], (16, embedded_ref.shape[1])).astype(jnp.bfloat16)
    for block in range(3):
        mod_out[:, block * width : (block + 1) * width] = dot(
            embedded, mod_buf[:, block * width : (block + 1) * width]
        )

    for k in range(np_):

        @pl.when(p == k)
        def _():
            for z in range(ns):
                start = z * rows + k * mine
                spot = slice(z * mine, (z + 1) * mine)
                embed_mine[:, spot] = embed_ref[:, start : start + mine]
                bias_mine[:, spot] = bias_ref[:, start : start + mine]
                gate_mine[:, spot] = mod_out[
                    0:1, 2 * width + start : 2 * width + start + mine
                ]
                final_mine[:, spot] = final_ref[:, start : start + mine]

    lat_all[p] = latent_ref[...]
    for d in range(1, np_):
        lat_copy(d, patch_of(np_ - d)).wait_recv()

    small = min(128, tokens)

    def norm_block(i, _):
        at = i * small
        owner = lax.div(at, tokens)
        inside = pl.multiple_of(lax.rem(at, tokens), small)
        latent = lat_all[owner, :, pl.ds(inside, small)].T.astype(jnp.bfloat16)
        hidden = dot(latent, embed_ref[...]) + bias_ref[...]
        centered = hidden - jnp.mean(hidden, axis=-1, keepdims=True)
        row_var = jnp.mean(centered * centered, axis=-1, keepdims=True)
        unit = centered * lax.rsqrt(row_var + epsilon)
        shifted = unit * (1.0 + mod_out[0:1, width : 2 * width]) + mod_out[0:1, 0:width]
        normed[pl.ds(pl.multiple_of(at, small), small), :] = shifted.astype(jnp.bfloat16)
        return 0

    lax.fori_loop(0, total // small, norm_block, 0)

    chunk = min(256, total)

    def project(owner, start, depth, first):
        def block(i, _):
            at = pl.ds(pl.multiple_of(i * chunk, chunk), chunk)
            lanes = pl.ds(pl.multiple_of(owner * rows + start, HEAD), depth)
            term = dot(
                normed[at, lanes],
                wq_buf[owner, pl.ds(pl.multiple_of(start, 16), depth), :],
            )
            raw[at, :] = term if first else raw[at, :] + term
            return 0

        lax.fori_loop(0, total // chunk, block, 0)

    loads[1].wait()
    project(s, 0, rows, True)
    for d in order:
        owner = step_of(ns - d)
        for c in range(cuts):
            wqz_copy(d, owner, c).wait_recv()
            if d is order[0]:
                wq_relay(c, begin)
            for e in range(1, nr):
                wqy_copy(d, e, r, c).start()
        if d is order[0]:
            each_direct(woz_copy, begin)
        project(owner, r * half, half, False)
    for d in order:
        owner = step_of(ns - d)
        for e in range(1, nr):
            other = rep_of(nr - e)
            for c in range(cuts):
                wqy_copy(d, e, other, c).wait_recv()
            project(owner, other * half, half, False)

    def norm_query(i, _):
        at = pl.ds(pl.multiple_of(i * chunk, chunk), chunk)
        for h in range(heads):
            q = raw[at, h * HEAD : (h + 1) * HEAD]
            q = q * lax.rsqrt(jnp.mean(q * q, axis=-1, keepdims=True) + epsilon) * gain_ref[...]
            queries[at, h * HEAD : (h + 1) * HEAD] = q.astype(jnp.bfloat16)
        return 0

    lax.fori_loop(0, total // chunk, norm_query, 0)

    loads[2].wait()
    loads[3].wait()
    for which in range(2):
        for d in range(1, np_):
            kv_copy(which, d, p, patch_of(np_ - d)).wait_recv()

    across = lax.rem(p + 2, np_)
    beside = p + 1 - 2 * lax.rem(p, 2)
    diagonal = lax.rem(beside + 2, np_)

    def head_copy(way, h, owner):
        spot = att.at[:, pl.ds(pl.multiple_of((owner * heads + h) * HEAD, HEAD), HEAD)]
        return send(
            spot,
            spot,
            att_s.at[way, h],
            att_r.at[way, h],
            {"patch": (across if way == 0 else beside)},
        )

    def pass_on(h):
        head_copy(0, h, across).wait_recv()
        head_copy(2, h, across).start()

    def wo_pass(d):
        for c in range(cuts):
            woz_copy(d, step_of(ns - d), c).wait_recv()
            if d is order[0]:
                wo_relay(c, begin)
            for e in range(1, nr):
                woy_copy(d, e, r, c).start()

    factor = 1.0 / math.sqrt(HEAD)
    for h in range(heads):

        def attend(i, _):
            at = pl.ds(pl.multiple_of(i * chunk, chunk), chunk)
            lanes = slice(h * HEAD, (h + 1) * HEAD)
            scores = dot(queries[at, lanes], key_buf[:, lanes], NT)
            peak = jnp.max(scores, axis=-1, keepdims=True)
            weights = jnp.exp((scores - peak) * factor)
            row_total = jnp.sum(weights, axis=-1, keepdims=True)
            blended = dot(weights.astype(jnp.bfloat16), value_buf[:, lanes]) / row_total
            spot = pl.ds(pl.multiple_of((p * heads + h) * HEAD, HEAD), HEAD)
            att[at, spot] = blended.astype(jnp.bfloat16)
            return 0

        lax.fori_loop(0, total // chunk, attend, 0)
        head_copy(0, h, p).start()
        head_copy(1, h, p).start()
        if h >= 1:
            pass_on(h - 1)
        if h == 0:
            wo_pass(order[0])

    for d in order[1:]:
        wo_pass(d)
    pass_on(heads - 1)
    for h in range(heads):
        head_copy(1, h, beside).wait_recv()
    loads[4].wait()
    for d in order:
        for e in range(1, nr):
            for c in range(cuts):
                woy_copy(d, e, rep_of(nr - e), c).wait_recv()
    pair = 2 * group
    chip = lax.div(p, 2)
    here = pl.ds(pl.multiple_of(chip * pair, HEAD), pair)
    there = pl.ds(pl.multiple_of((1 - chip) * pair, HEAD), pair)

    def near(i, _):
        at = pl.ds(pl.multiple_of(i * chunk, chunk), chunk)
        branch[at, :] = dot(att[at, here], wo_buf[:, here], NT)
        return 0

    lax.fori_loop(0, total // chunk, near, 0)
    for h in range(heads):
        head_copy(2, h, diagonal).wait_recv()

    own_sum = dot(jnp.ones((16, feats), jnp.bfloat16), final_mine[...], NT)[0:1]

    def partner(d):
        return jnp.where(d == 1, across, jnp.where(d == 2, diagonal, jnp.where(d == 3, beside, p)))

    def finish(d):
        owner = partner(d)
        at = pl.ds(pl.multiple_of(owner * tokens, tokens), tokens)
        full = branch[at, :] + dot(att[at, there], wo_buf[:, there], NT)
        latent = lat_all[owner].T.astype(jnp.bfloat16)
        hidden = dot(latent, embed_mine[...]) + bias_mine[...]
        mixed = hidden + gate_mine[...] * full
        middle = jnp.mean(mixed, axis=-1, keepdims=True)
        centered = mixed - middle
        spread = jnp.sum(centered * centered, axis=-1, keepdims=True)
        lane = lax.broadcasted_iota(jnp.int32, (tokens, channels), 1)
        pay[d, :, 0:channels] = (
            dot(centered.astype(jnp.bfloat16), final_mine[...], NT) + middle * own_sum
        )
        pay[d, :, channels : 2 * channels] = jnp.where(lane < channels // 2, middle, spread)

    def pay_copy(d):
        return send(
            pay.at[d], pay_in.at[d], pay_s.at[d], pay_r.at[d], {"patch": partner(d)}
        )

    def finish_other(d, _):
        finish(d)
        pay_copy(d).start()
        return 0

    lax.fori_loop(1, np_, finish_other, 0)
    finish(0)
    for d in range(1, np_):
        pay_copy(d).wait_recv()
    every = [pay[0]] + [pay_in[d] for d in range(1, np_)]
    product = sum(item[:, 0:channels] for item in every)
    middles = [item[:, channels : channels + 1] for item in every]
    row_mean = sum(middles) / np_
    spread = sum(
        item[:, channels + channels // 2 : channels + channels // 2 + 1]
        + feats * (middle - row_mean) * (middle - row_mean)
        for item, middle in zip(every, middles)
    )
    all_sum = dot(jnp.ones((16, width), jnp.bfloat16), final_ref[...], NT)[0:1]
    velocity = (product - row_mean * all_sum) * lax.rsqrt(spread / width + epsilon)
    drift = velocity * dt_ref[0:1, 0:1]
    drift_out[...] = drift.astype(jnp.bfloat16)

    def drift_copy(d):
        return send(
            drift_out, drift_in.at[d], dr_s.at[d], dr_r.at[d], {"step": step_of(d)}
        )

    for d in range(1, ns):

        @pl.when(s + d < ns)
        def _():
            drift_copy(d).start()

    drift_sum[...] = drift
    for d in range(1, ns):

        @pl.when(s - d >= 0)
        def _():
            drift_copy(d).wait_recv()
            drift_sum[...] += drift_in[d].astype(jnp.float32)

    out_ref[...] = noise_ref[...] + drift_sum[...].T

    for d in range(1, np_):
        lat_copy(d, p).wait_send()
        pay_copy(d).wait_send()
        for which in range(2):
            kv_copy(which, d, patch_of(d), p).wait_send()
    each_direct(wqz_copy, sent)
    each_direct(woz_copy, sent)
    for c in range(cuts):
        wq_relay(c, sent)
        wo_relay(c, sent)
    for d in range(1, ns):
        for e in range(1, nr):
            for c in range(cuts):
                wqy_copy(d, e, r, c).wait_send()
                woy_copy(d, e, r, c).wait_send()

        @pl.when(s + d < ns)
        def _():
            drift_copy(d).wait_send()

    for h in range(heads):
        head_copy(0, h, p).wait_send()
        head_copy(1, h, p).wait_send()
        head_copy(2, h, across).wait_send()


def fused_device(
    sizes,
    latent_old,
    noise_start,
    step_index,
    sigma_table,
    mod_weight,
    embed_weight,
    embed_bias,
    query_weight,
    query_gain,
    stale_keys,
    stale_values,
    out_weight,
    final_weight,
):
    nr, ns, np_ = sizes
    step_slot = step_index[0]
    table_slots = jnp.arange(sigma_table.shape[0])
    sigma_now = jnp.sum(jnp.where(table_slots == step_slot, sigma_table, 0.0))
    sigma_next = jnp.sum(jnp.where(table_slots == step_slot + 1, sigma_table, 0.0))
    embedded = jax.nn.silu(time_embed(sigma_now)).astype(jnp.bfloat16)
    embedded = embedded.astype(jnp.float32)[None, :]
    dt = (sigma_next - sigma_now).reshape(1, 1)
    tokens, channels = latent_old.shape[1:]
    width = embed_weight.shape[1]
    rows, inner = query_weight.shape
    keys = stale_keys.shape[1]
    group = inner // np_
    heads = group // HEAD
    feats = width // np_
    total = tokens * np_
    bf, f32 = jnp.bfloat16, jnp.float32
    dma = pltpu.SemaphoreType.DMA
    vmem = pl.BlockSpec(memory_space=pltpu.VMEM)
    anywhere = pl.BlockSpec(memory_space=pl.ANY)
    out = pl.pallas_call(
        functools.partial(fused_kernel, sizes),
        out_shape=jax.ShapeDtypeStruct((channels, tokens), f32),
        in_specs=[vmem] * 8 + [anywhere] * 5,
        out_specs=vmem,
        scratch_shapes=[
            pltpu.VMEM((np_, channels, tokens), f32),
            pltpu.VMEM(mod_weight.shape, bf),
            pltpu.VMEM((16, 3 * width), f32),
            pltpu.VMEM((ns, rows, group), bf),
            pltpu.VMEM((np_ * keys, group), bf),
            pltpu.VMEM((np_ * keys, group), bf),
            pltpu.VMEM((feats, inner), bf),
            pltpu.VMEM((total, width), bf),
            pltpu.VMEM((total, group), f32),
            pltpu.VMEM((total, group), bf),
            pltpu.VMEM((total, inner), bf),
            pltpu.VMEM((total, feats), f32),
            pltpu.VMEM((channels, feats), bf),
            pltpu.VMEM((1, feats), f32),
            pltpu.VMEM((1, feats), f32),
            pltpu.VMEM((channels, feats), bf),
            pltpu.VMEM((np_, tokens, 2 * channels), f32),
            pltpu.VMEM((np_, tokens, 2 * channels), f32),
            pltpu.VMEM((tokens, channels), bf),
            pltpu.VMEM((ns, tokens, channels), bf),
            pltpu.VMEM((tokens, channels), f32),
            dma((5,)),
            dma((np_,)),
            dma((np_,)),
            dma((2, np_)),
            dma((2, np_)),
            dma((ns, CUTS)),
            dma((ns, CUTS)),
            dma((ns, nr, CUTS)),
            dma((ns, nr, CUTS)),
            dma((ns, CUTS)),
            dma((ns, CUTS)),
            dma((ns, nr, CUTS)),
            dma((ns, nr, CUTS)),
            dma((3, heads)),
            dma((3, heads)),
            dma((np_,)),
            dma((np_,)),
            dma((ns,)),
            dma((ns,)),
        ],
        compiler_params=pltpu.CompilerParams(
            collective_id=0, has_side_effects=True, vmem_limit_bytes=60 * 1024 * 1024
        ),
    )(
        latent_old[0].T,
        noise_start.T,
        embedded,
        dt,
        embed_weight,
        embed_bias[None, :],
        query_gain[None, :],
        final_weight.T,
        mod_weight,
        query_weight,
        stale_keys[0],
        stale_values[0],
        out_weight,
    )
    return out.T[None]


def fits(mesh):
    nr, ns, np_ = (mesh.shape[axis] for axis in ("rep", "step", "patch"))
    return np_ == 4 and ns <= 4 and D % (ns * np_ * nr * CUTS * 16) == 0 and D // (ns * nr) % HEAD == 0


def solution(mesh):
    placed = (
        P(("rep", "step"), "patch", None),
        P(("rep", "patch"), None),
        P(("rep", "step")),
        P(),
        P(),
        P(),
        P(),
        P("step", None),
        P(),
        P(("rep", "step"), "patch", None),
        P(("rep", "step"), "patch", None),
        P("step", None),
        P(),
    )
    sizes = tuple(mesh.shape[axis] for axis in ("rep", "step", "patch"))
    per_device = functools.partial(fused_device, sizes) if fits(mesh) else plain_device
    return jax.shard_map(
        per_device,
        mesh=mesh,
        in_specs=placed,
        out_specs=P(("rep", "step"), "patch", None),
        check_vma=False,
    )
```

```python
import functools
import math

import jax
import jax.numpy as jnp
from jax import lax
from jax.experimental import pallas as pl
from jax.experimental.pallas import tpu as pltpu
from jax.sharding import PartitionSpec as P

D = 3072
HEAD = 128
FREQ = 256
HEADS = 12


epsilon = 1e-06
CUTS = 1


def entering(shard, axis, join, neutral):
    place = lax.axis_index(axis)
    gathered = lax.all_gather(shard.astype(jnp.bfloat16), axis)
    state = jnp.zeros_like(shard) + jnp.asarray(neutral, shard.dtype)

    def one(hop, state):
        return join(state, lax.dynamic_index_in_dim(gathered, hop, 0, False).astype(shard.dtype))

    return lax.fori_loop(0, place, one, state)


def layer_norm(values_in):
    row_mean = jnp.mean(values_in, axis=-1, keepdims=True)
    centered = values_in - row_mean
    row_var = jnp.mean(centered * centered, axis=-1, keepdims=True)
    return centered * lax.rsqrt(row_var + epsilon)


def time_embed(sigma_now):
    half_count = FREQ // 2
    frequency = jnp.exp(
        -math.log(10000.0) * jnp.arange(half_count).astype(jnp.float32) / half_count
    )
    angles = 1000.0 * sigma_now * frequency
    return jnp.concatenate([jnp.cos(angles), jnp.sin(angles)])


def project_back(attended, weight_rows):
    return lax.dot_general(
        attended, weight_rows, (((1,), (1,)), ((), ())), preferred_element_type=jnp.float32
    )


def norm_queries(raw_queries, query_gain):
    token_count = raw_queries.shape[0]
    head_count = raw_queries.shape[1] // HEAD
    queries = raw_queries.reshape(token_count, head_count, HEAD)
    queries = (
        queries
        * lax.rsqrt(jnp.mean(queries * queries, axis=-1, keepdims=True) + epsilon)
        * query_gain
    )
    return queries.astype(jnp.bfloat16)


def empty_state(queries):
    token_count = queries.shape[0]
    head_count = queries.shape[1]
    return (
        jnp.full((head_count, token_count), -jnp.inf, jnp.float32),
        jnp.zeros((head_count, token_count), jnp.float32),
        jnp.zeros((head_count, token_count, HEAD), jnp.float32),
    )


def attend_block(queries, state_tuple, key_piece, value_piece):
    head_count = queries.shape[1]
    row_count = key_piece.shape[0]
    key_split = key_piece.reshape(row_count, head_count, HEAD)
    value_split = value_piece.reshape(row_count, head_count, HEAD)
    run_peak, run_total, run_sum = state_tuple
    scores = jnp.einsum(
        "qhd,khd->hqk", queries, key_split, preferred_element_type=jnp.float32
    ) / math.sqrt(HEAD)
    new_peak = jnp.max(scores, axis=-1)
    rescale = jnp.exp(run_peak - new_peak)
    exp_weights = jnp.exp(scores - new_peak[..., None])
    run_total = run_total * rescale + jnp.sum(exp_weights, axis=-1)
    run_sum = run_sum * rescale[..., None] + jnp.einsum(
        "hqk,khd->hqd",
        exp_weights.astype(jnp.bfloat16),
        value_split,
        preferred_element_type=jnp.float32,
    )
    return (new_peak, run_total, run_sum)


def finish_heads(state_tuple):
    final_peak, final_total, final_sum = state_tuple
    blended = final_sum / final_total[..., None]
    token_count = blended.shape[1]
    return jnp.transpose(blended, (1, 0, 2)).reshape(token_count, -1).astype(jnp.bfloat16)


def plain_device(
    latent_old,
    noise_start,
    step_index,
    sigma_table,
    mod_weight,
    embed_weight,
    embed_bias,
    query_weight,
    query_gain,
    stale_keys,
    stale_values,
    out_weight,
    final_weight,
):
    step_slot = step_index[0]
    table_slots = jnp.arange(sigma_table.shape[0])
    sigma_now = jnp.sum(jnp.where(table_slots == step_slot, sigma_table, 0.0))
    sigma_next = jnp.sum(jnp.where(table_slots == step_slot + 1, sigma_table, 0.0))
    embedded = jax.nn.silu(time_embed(sigma_now)).astype(jnp.bfloat16)
    modulate = jnp.dot(embedded[None, :], mod_weight, preferred_element_type=jnp.float32)[0]
    width = D
    shift_vec = modulate[:width]
    scale_vec = modulate[width : 2 * width]
    gate_vec = modulate[2 * width :]
    latent = latent_old[0]
    token_count = latent.shape[0]
    hidden = (
        jnp.dot(latent.astype(jnp.bfloat16), embed_weight, preferred_element_type=jnp.float32)
        + embed_bias
    )
    normed = (layer_norm(hidden) * (1.0 + scale_vec) + shift_vec).astype(jnp.bfloat16)
    patch_count = lax.axis_size("patch")
    group_width = HEADS // patch_count * HEAD
    patch_slot = lax.axis_index("patch")
    query_columns = lax.dynamic_slice_in_dim(query_weight, patch_slot * group_width, group_width, 1)
    normed_every = lax.all_gather(normed, "patch", axis=0, tiled=True)
    raw_every = jnp.dot(
        normed_every,
        lax.all_gather(query_columns, "step", axis=0, tiled=True),
        preferred_element_type=jnp.float32,
    )
    queries_every = norm_queries(raw_every, query_gain)
    keys_group, values_group = (
        lax.all_to_all(stale_keys[0], "patch", split_axis=1, concat_axis=0, tiled=True),
        lax.all_to_all(stale_values[0], "patch", split_axis=1, concat_axis=0, tiled=True),
    )
    state_every = attend_block(queries_every, empty_state(queries_every), keys_group, values_group)
    attended_every = finish_heads(state_every)
    attended = lax.all_to_all(attended_every, "patch", split_axis=0, concat_axis=1, tiled=True)
    branch = project_back(attended, lax.all_gather(out_weight, "step", axis=0, tiled=True))
    mixed = hidden + gate_vec * branch
    velocity = jnp.dot(
        layer_norm(mixed).astype(jnp.bfloat16), final_weight, preferred_element_type=jnp.float32
    )
    drift_term = velocity * (sigma_next - sigma_now)
    flat_term = drift_term.reshape(-1, 128)

    def add_terms(earlier, later):
        return earlier + later

    prefix = entering(flat_term, "step", add_terms, jnp.zeros_like(flat_term))
    result = noise_start + (prefix + flat_term).reshape(token_count, -1)
    return result[None]


NT = (((1,), (1,)), ((), ()))
NN = (((1,), (0,)), ((), ()))


def send(src, dst, send_sem, recv_sem, target):
    return pltpu.make_async_remote_copy(
        src_ref=src,
        dst_ref=dst,
        send_sem=send_sem,
        recv_sem=recv_sem,
        device_id=target,
        device_id_type=pl.DeviceIdType.MESH,
    )


def dot(a, b, dims=NN):
    return lax.dot_general(a, b, dims, preferred_element_type=jnp.float32)


def fused_kernel(
    sizes,
    latent_ref,
    noise_ref,
    embedded_ref,
    dt_ref,
    embed_ref,
    bias_ref,
    gain_ref,
    final_ref,
    mod_hbm,
    wq_hbm,
    key_hbm,
    value_hbm,
    wo_hbm,
    out_ref,
    lat_all,
    mod_buf,
    mod_out,
    wq_buf,
    key_buf,
    value_buf,
    wo_buf,
    normed,
    raw,
    queries,
    att,
    branch,
    embed_mine,
    bias_mine,
    gate_mine,
    final_mine,
    pay,
    pay_in,
    drift_out,
    drift_in,
    drift_sum,
    local_sem,
    lat_s,
    lat_r,
    kv_s,
    kv_r,
    wqz_s,
    wqz_r,
    wqy_s,
    wqy_r,
    woz_s,
    woz_r,
    woy_s,
    woy_r,
    att_s,
    att_r,
    pay_s,
    pay_r,
    dr_s,
    dr_r,
):
    nr, ns, np_ = sizes
    r, s, p = lax.axis_index("rep"), lax.axis_index("step"), lax.axis_index("patch")
    channels, tokens = latent_ref.shape
    total = tokens * np_
    width = embed_ref.shape[1]
    rows = wq_hbm.shape[0]
    inner = wq_hbm.shape[1]
    group = inner // np_
    heads = group // HEAD
    keys = key_hbm.shape[0]
    half = rows // nr
    mine = rows // np_
    part = mine // nr
    feats = width // np_
    cuts = CUTS
    half_cut = half // cuts
    part_cut = part // cuts

    def patch_of(d):
        return lax.rem(p + d, np_)

    def step_of(d):
        return lax.rem(s + d, ns)

    def rep_of(d):
        return lax.rem(r + d, nr)

    loads = [
        pltpu.make_async_copy(mod_hbm, mod_buf, local_sem.at[0]),
        pltpu.make_async_copy(
            wq_hbm.at[:, pl.ds(pl.multiple_of(p * group, HEAD), group)],
            wq_buf.at[s],
            local_sem.at[1],
        ),
        pltpu.make_async_copy(
            key_hbm.at[:, pl.ds(pl.multiple_of(p * group, HEAD), group)],
            key_buf.at[pl.ds(pl.multiple_of(p * keys, 16), keys), :],
            local_sem.at[2],
        ),
        pltpu.make_async_copy(
            value_hbm.at[:, pl.ds(pl.multiple_of(p * group, HEAD), group)],
            value_buf.at[pl.ds(pl.multiple_of(p * keys, 16), keys), :],
            local_sem.at[3],
        ),
        pltpu.make_async_copy(
            wo_hbm.at[pl.ds(pl.multiple_of(p * mine, 16), mine), :],
            wo_buf.at[pl.ds(pl.multiple_of(s * mine, 16), mine), :],
            local_sem.at[4],
        ),
    ]
    barrier = pltpu.get_barrier_semaphore()
    for d in range(1, np_):
        pl.semaphore_signal(
            barrier, inc=1, device_id={"patch": patch_of(d)}, device_id_type=pl.DeviceIdType.MESH
        )
    for d in range(1, ns):
        pl.semaphore_signal(
            barrier, inc=1, device_id={"step": step_of(d)}, device_id_type=pl.DeviceIdType.MESH
        )
    for d in range(1, nr):
        pl.semaphore_signal(
            barrier, inc=1, device_id={"rep": rep_of(d)}, device_id_type=pl.DeviceIdType.MESH
        )
    for load in loads:
        load.start()
    pl.semaphore_wait(barrier, np_ - 1 + ns - 1 + nr - 1)

    def lat_copy(d, owner):
        return send(
            latent_ref, lat_all.at[owner], lat_s.at[d], lat_r.at[d], {"patch": patch_of(d)}
        )

    def kv_copy(which, d, taker, owner):
        source = (key_hbm, value_hbm)[which]
        target = (key_buf, value_buf)[which]
        return send(
            source.at[:, pl.ds(pl.multiple_of(taker * group, HEAD), group)],
            target.at[pl.ds(pl.multiple_of(owner * keys, 16), keys), :],
            kv_s.at[which, d],
            kv_r.at[which, d],
            {"patch": taker},
        )

    def wq_rows(from_rep, c):
        return pl.ds(pl.multiple_of(from_rep * half + c * half_cut, 16), half_cut)

    def wo_rows(base, from_rep, c):
        return pl.ds(pl.multiple_of(base * mine + from_rep * part + c * part_cut, 16), part_cut)

    def wqz_copy(d, owner, c):
        return send(
            wq_hbm.at[wq_rows(r, c), pl.ds(pl.multiple_of(p * group, HEAD), group)],
            wq_buf.at[owner, wq_rows(r, c), :],
            wqz_s.at[d, c],
            wqz_r.at[d, c],
            {"step": step_of(d)},
        )

    def wqy_copy(d, e, from_rep, c):
        spot = wq_buf.at[step_of(ns - d), wq_rows(from_rep, c), :]
        return send(spot, spot, wqy_s.at[d, e, c], wqy_r.at[d, e, c], {"rep": rep_of(e)})

    def woz_copy(d, owner, c):
        return send(
            wo_hbm.at[wo_rows(p, r, c), :],
            wo_buf.at[wo_rows(owner, r, c), :],
            woz_s.at[d, c],
            woz_r.at[d, c],
            {"step": step_of(d)},
        )

    def woy_copy(d, e, from_rep, c):
        spot = wo_buf.at[wo_rows(step_of(ns - d), from_rep, c), :]
        return send(spot, spot, woy_s.at[d, e, c], woy_r.at[d, e, c], {"rep": rep_of(e)})

    for d in range(1, np_):
        lat_copy(d, p).start()
    relayed = ns == 4
    if relayed:
        early = 3 - 2 * jnp.minimum(s, 1)
        order = [2, early, 4 - early]
    else:
        order = list(range(1, ns))

    def each_direct(copy, act):
        for d in [2, 1, 3] if relayed else order:
            for c in range(cuts):
                if relayed and d != 2:

                    @pl.when(s != (0 if d == 3 else ns - 1))
                    def _():
                        act(copy(d, s, c))

                else:
                    act(copy(d, s, c))

    def relay(spot, send_sem, recv_sem, c, act):
        if relayed:
            for place, target, d in ((2, 3, 3), (1, 0, 1)):

                @pl.when(s == place)
                def _():
                    act(send(spot, spot, send_sem.at[0, c], recv_sem.at[d, c], {"step": target}))

    def wq_relay(c, act):
        relay(wq_buf.at[step_of(ns - 2), wq_rows(r, c), :], wqz_s, wqz_r, c, act)

    def wo_relay(c, act):
        relay(wo_buf.at[wo_rows(step_of(ns - 2), r, c), :], woz_s, woz_r, c, act)

    def begin(copy):
        copy.start()

    def sent(copy):
        copy.wait_send()

    each_direct(wqz_copy, begin)
    for which in range(2):
        for d in range(1, np_):
            kv_copy(which, d, patch_of(d), p).start()
    loads[0].wait()
    embedded = jnp.broadcast_to(embedded_ref[...], (16, embedded_ref.shape[1])).astype(jnp.bfloat16)
    for block in range(3):
        mod_out[:, block * width : (block + 1) * width] = dot(
            embedded, mod_buf[:, block * width : (block + 1) * width]
        )

    for k in range(np_):

        @pl.when(p == k)
        def _():
            for z in range(ns):
                start = z * rows + k * mine
                spot = slice(z * mine, (z + 1) * mine)
                embed_mine[:, spot] = embed_ref[:, start : start + mine]
                bias_mine[:, spot] = bias_ref[:, start : start + mine]
                gate_mine[:, spot] = mod_out[
                    0:1, 2 * width + start : 2 * width + start + mine
                ]
                final_mine[:, spot] = final_ref[:, start : start + mine]

    lat_all[p] = latent_ref[...]
    for d in range(1, np_):
        lat_copy(d, patch_of(np_ - d)).wait_recv()

    small = min(128, tokens)

    def norm_block(i, _):
        at = i * small
        owner = lax.div(at, tokens)
        inside = pl.multiple_of(lax.rem(at, tokens), small)
        latent = lat_all[owner, :, pl.ds(inside, small)].T.astype(jnp.bfloat16)
        hidden = dot(latent, embed_ref[...]) + bias_ref[...]
        centered = hidden - jnp.mean(hidden, axis=-1, keepdims=True)
        row_var = jnp.mean(centered * centered, axis=-1, keepdims=True)
        unit = centered * lax.rsqrt(row_var + epsilon)
        shifted = unit * (1.0 + mod_out[0:1, width : 2 * width]) + mod_out[0:1, 0:width]
        normed[pl.ds(pl.multiple_of(at, small), small), :] = shifted.astype(jnp.bfloat16)
        return 0

    lax.fori_loop(0, total // small, norm_block, 0)

    chunk = min(256, total)

    def project(owner, start, depth, first):
        def block(i, _):
            at = pl.ds(pl.multiple_of(i * chunk, chunk), chunk)
            lanes = pl.ds(pl.multiple_of(owner * rows + start, HEAD), depth)
            term = dot(
                normed[at, lanes],
                wq_buf[owner, pl.ds(pl.multiple_of(start, 16), depth), :],
            )
            raw[at, :] = term if first else raw[at, :] + term
            return 0

        lax.fori_loop(0, total // chunk, block, 0)

    loads[1].wait()
    project(s, 0, rows, True)
    for d in order:
        owner = step_of(ns - d)
        for c in range(cuts):
            wqz_copy(d, owner, c).wait_recv()
            if d is order[0]:
                wq_relay(c, begin)
            for e in range(1, nr):
                wqy_copy(d, e, r, c).start()
        if d is order[0]:
            each_direct(woz_copy, begin)
        project(owner, r * half, half, False)
    for d in order:
        owner = step_of(ns - d)
        for e in range(1, nr):
            other = rep_of(nr - e)
            for c in range(cuts):
                wqy_copy(d, e, other, c).wait_recv()
            project(owner, other * half, half, False)

    def norm_query(i, _):
        at = pl.ds(pl.multiple_of(i * chunk, chunk), chunk)
        for h in range(heads):
            q = raw[at, h * HEAD : (h + 1) * HEAD]
            q = q * lax.rsqrt(jnp.mean(q * q, axis=-1, keepdims=True) + epsilon) * gain_ref[...]
            queries[at, h * HEAD : (h + 1) * HEAD] = q.astype(jnp.bfloat16)
        return 0

    lax.fori_loop(0, total // chunk, norm_query, 0)

    loads[2].wait()
    loads[3].wait()
    for which in range(2):
        for d in range(1, np_):
            kv_copy(which, d, p, patch_of(np_ - d)).wait_recv()

    across = lax.rem(p + 2, np_)
    beside = p + 1 - 2 * lax.rem(p, 2)
    diagonal = lax.rem(beside + 2, np_)

    def head_copy(way, h, owner):
        spot = att.at[:, pl.ds(pl.multiple_of((owner * heads + h) * HEAD, HEAD), HEAD)]
        return send(
            spot,
            spot,
            att_s.at[way, h],
            att_r.at[way, h],
            {"patch": (across if way == 0 else beside)},
        )

    def pass_on(h):
        head_copy(0, h, across).wait_recv()
        head_copy(2, h, across).start()

    def wo_pass(d):
        for c in range(cuts):
            woz_copy(d, step_of(ns - d), c).wait_recv()
            if d is order[0]:
                wo_relay(c, begin)
            for e in range(1, nr):
                woy_copy(d, e, r, c).start()

    factor = 1.0 / math.sqrt(HEAD)
    for h in range(heads):

        def attend(i, _):
            at = pl.ds(pl.multiple_of(i * chunk, chunk), chunk)
            lanes = slice(h * HEAD, (h + 1) * HEAD)
            scores = dot(queries[at, lanes], key_buf[:, lanes], NT)
            peak = jnp.max(scores, axis=-1, keepdims=True)
            weights = jnp.exp((scores - peak) * factor)
            row_total = jnp.sum(weights, axis=-1, keepdims=True)
            blended = dot(weights.astype(jnp.bfloat16), value_buf[:, lanes]) / row_total
            spot = pl.ds(pl.multiple_of((p * heads + h) * HEAD, HEAD), HEAD)
            att[at, spot] = blended.astype(jnp.bfloat16)
            return 0

        lax.fori_loop(0, total // chunk, attend, 0)
        head_copy(0, h, p).start()
        head_copy(1, h, p).start()
        if h >= 1:
            pass_on(h - 1)
        if h == 0:
            wo_pass(order[0])
        if h == 1:
            wo_pass(order[1])

    for d in order[2:]:
        wo_pass(d)
    pass_on(heads - 1)
    for h in range(heads):
        head_copy(1, h, beside).wait_recv()
    loads[4].wait()
    for d in order:
        for e in range(1, nr):
            for c in range(cuts):
                woy_copy(d, e, rep_of(nr - e), c).wait_recv()
    pair = 2 * group
    chip = lax.div(p, 2)
    here = pl.ds(pl.multiple_of(chip * pair, HEAD), pair)
    there = pl.ds(pl.multiple_of((1 - chip) * pair, HEAD), pair)

    def near(i, _):
        at = pl.ds(pl.multiple_of(i * chunk, chunk), chunk)
        branch[at, :] = dot(att[at, here], wo_buf[:, here], NT)
        return 0

    lax.fori_loop(0, total // chunk, near, 0)
    for h in range(heads):
        head_copy(2, h, diagonal).wait_recv()

    own_sum = dot(jnp.ones((16, feats), jnp.bfloat16), final_mine[...], NT)[0:1]

    def partner(d):
        return jnp.where(d == 1, across, jnp.where(d == 2, diagonal, jnp.where(d == 3, beside, p)))

    def finish(d):
        owner = partner(d)
        at = pl.ds(pl.multiple_of(owner * tokens, tokens), tokens)
        full = branch[at, :] + dot(att[at, there], wo_buf[:, there], NT)
        latent = lat_all[owner].T.astype(jnp.bfloat16)
        hidden = dot(latent, embed_mine[...]) + bias_mine[...]
        mixed = hidden + gate_mine[...] * full
        middle = jnp.mean(mixed, axis=-1, keepdims=True)
        centered = mixed - middle
        spread = jnp.sum(centered * centered, axis=-1, keepdims=True)
        lane = lax.broadcasted_iota(jnp.int32, (tokens, channels), 1)
        pay[d, :, 0:channels] = (
            dot(centered.astype(jnp.bfloat16), final_mine[...], NT) + middle * own_sum
        )
        pay[d, :, channels : 2 * channels] = jnp.where(lane < channels // 2, middle, spread)

    def pay_copy(d):
        return send(
            pay.at[d], pay_in.at[d], pay_s.at[d], pay_r.at[d], {"patch": partner(d)}
        )

    def finish_other(d, _):
        finish(d)
        pay_copy(d).start()
        return 0

    lax.fori_loop(1, np_, finish_other, 0)
    finish(0)
    for d in range(1, np_):
        pay_copy(d).wait_recv()
    every = [pay[0]] + [pay_in[d] for d in range(1, np_)]
    product = sum(item[:, 0:channels] for item in every)
    middles = [item[:, channels : channels + 1] for item in every]
    row_mean = sum(middles) / np_
    spread = sum(
        item[:, channels + channels // 2 : channels + channels // 2 + 1]
        + feats * (middle - row_mean) * (middle - row_mean)
        for item, middle in zip(every, middles)
    )
    all_sum = dot(jnp.ones((16, width), jnp.bfloat16), final_ref[...], NT)[0:1]
    velocity = (product - row_mean * all_sum) * lax.rsqrt(spread / width + epsilon)
    drift = velocity * dt_ref[0:1, 0:1]
    drift_out[...] = drift.astype(jnp.bfloat16)

    def drift_copy(d):
        return send(
            drift_out, drift_in.at[d], dr_s.at[d], dr_r.at[d], {"step": step_of(d)}
        )

    for d in range(1, ns):

        @pl.when(s + d < ns)
        def _():
            drift_copy(d).start()

    drift_sum[...] = drift
    for d in range(1, ns):

        @pl.when(s - d >= 0)
        def _():
            drift_copy(d).wait_recv()
            drift_sum[...] += drift_in[d].astype(jnp.float32)

    out_ref[...] = noise_ref[...] + drift_sum[...].T

    for d in range(1, np_):
        lat_copy(d, p).wait_send()
        pay_copy(d).wait_send()
        for which in range(2):
            kv_copy(which, d, patch_of(d), p).wait_send()
    each_direct(wqz_copy, sent)
    each_direct(woz_copy, sent)
    for c in range(cuts):
        wq_relay(c, sent)
        wo_relay(c, sent)
    for d in range(1, ns):
        for e in range(1, nr):
            for c in range(cuts):
                wqy_copy(d, e, r, c).wait_send()
                woy_copy(d, e, r, c).wait_send()

        @pl.when(s + d < ns)
        def _():
            drift_copy(d).wait_send()

    for h in range(heads):
        head_copy(0, h, p).wait_send()
        head_copy(1, h, p).wait_send()
        head_copy(2, h, across).wait_send()


def fused_device(
    sizes,
    latent_old,
    noise_start,
    step_index,
    sigma_table,
    mod_weight,
    embed_weight,
    embed_bias,
    query_weight,
    query_gain,
    stale_keys,
    stale_values,
    out_weight,
    final_weight,
):
    nr, ns, np_ = sizes
    step_slot = step_index[0]
    table_slots = jnp.arange(sigma_table.shape[0])
    sigma_now = jnp.sum(jnp.where(table_slots == step_slot, sigma_table, 0.0))
    sigma_next = jnp.sum(jnp.where(table_slots == step_slot + 1, sigma_table, 0.0))
    embedded = jax.nn.silu(time_embed(sigma_now)).astype(jnp.bfloat16)
    embedded = embedded.astype(jnp.float32)[None, :]
    dt = (sigma_next - sigma_now).reshape(1, 1)
    tokens, channels = latent_old.shape[1:]
    width = embed_weight.shape[1]
    rows, inner = query_weight.shape
    keys = stale_keys.shape[1]
    group = inner // np_
    heads = group // HEAD
    feats = width // np_
    total = tokens * np_
    bf, f32 = jnp.bfloat16, jnp.float32
    dma = pltpu.SemaphoreType.DMA
    vmem = pl.BlockSpec(memory_space=pltpu.VMEM)
    anywhere = pl.BlockSpec(memory_space=pl.ANY)
    out = pl.pallas_call(
        functools.partial(fused_kernel, sizes),
        out_shape=jax.ShapeDtypeStruct((channels, tokens), f32),
        in_specs=[vmem] * 8 + [anywhere] * 5,
        out_specs=vmem,
        scratch_shapes=[
            pltpu.VMEM((np_, channels, tokens), f32),
            pltpu.VMEM(mod_weight.shape, bf),
            pltpu.VMEM((16, 3 * width), f32),
            pltpu.VMEM((ns, rows, group), bf),
            pltpu.VMEM((np_ * keys, group), bf),
            pltpu.VMEM((np_ * keys, group), bf),
            pltpu.VMEM((feats, inner), bf),
            pltpu.VMEM((total, width), bf),
            pltpu.VMEM((total, group), f32),
            pltpu.VMEM((total, group), bf),
            pltpu.VMEM((total, inner), bf),
            pltpu.VMEM((total, feats), f32),
            pltpu.VMEM((channels, feats), bf),
            pltpu.VMEM((1, feats), f32),
            pltpu.VMEM((1, feats), f32),
            pltpu.VMEM((channels, feats), bf),
            pltpu.VMEM((np_, tokens, 2 * channels), f32),
            pltpu.VMEM((np_, tokens, 2 * channels), f32),
            pltpu.VMEM((tokens, channels), bf),
            pltpu.VMEM((ns, tokens, channels), bf),
            pltpu.VMEM((tokens, channels), f32),
            dma((5,)),
            dma((np_,)),
            dma((np_,)),
            dma((2, np_)),
            dma((2, np_)),
            dma((ns, CUTS)),
            dma((ns, CUTS)),
            dma((ns, nr, CUTS)),
            dma((ns, nr, CUTS)),
            dma((ns, CUTS)),
            dma((ns, CUTS)),
            dma((ns, nr, CUTS)),
            dma((ns, nr, CUTS)),
            dma((3, heads)),
            dma((3, heads)),
            dma((np_,)),
            dma((np_,)),
            dma((ns,)),
            dma((ns,)),
        ],
        compiler_params=pltpu.CompilerParams(
            collective_id=0, has_side_effects=True, vmem_limit_bytes=60 * 1024 * 1024
        ),
    )(
        latent_old[0].T,
        noise_start.T,
        embedded,
        dt,
        embed_weight,
        embed_bias[None, :],
        query_gain[None, :],
        final_weight.T,
        mod_weight,
        query_weight,
        stale_keys[0],
        stale_values[0],
        out_weight,
    )
    return out.T[None]


def fits(mesh):
    nr, ns, np_ = (mesh.shape[axis] for axis in ("rep", "step", "patch"))
    return np_ == 4 and ns <= 4 and D % (ns * np_ * nr * CUTS * 16) == 0 and D // (ns * nr) % HEAD == 0


def solution(mesh):
    placed = (
        P(("rep", "step"), "patch", None),
        P(("rep", "patch"), None),
        P(("rep", "step")),
        P(),
        P(),
        P(),
        P(),
        P("step", None),
        P(),
        P(("rep", "step"), "patch", None),
        P(("rep", "step"), "patch", None),
        P("step", None),
        P(),
    )
    sizes = tuple(mesh.shape[axis] for axis in ("rep", "step", "patch"))
    per_device = functools.partial(fused_device, sizes) if fits(mesh) else plain_device
    return jax.shard_map(
        per_device,
        mesh=mesh,
        in_specs=placed,
        out_specs=P(("rep", "step"), "patch", None),
        check_vma=False,
    )
```
